512 devices in a mesh: ctx: 64 (over z, x, core), head: 8 (over y).
Axes of the slice: x: 4, y: 8, z: 8, core: 2. Of those that a mesh axis runs over, the one named last changes fastest.
Arguments:
- queries: bfloat16 [16384, 4096], P(('ctx', 'head')), may hold values from -6 to 6
- key_rows: bfloat16 [16384, 4096], P(('ctx', 'head')), may hold values from -6 to 6
- value_rows: bfloat16 [16384, 4096], P(('ctx', 'head')), may hold values from -6 to 6
- grad_out: bfloat16 [16384, 4096], P(('ctx', 'head')), may hold values from -6 to 6
Outputs:
- grad_query: bfloat16 [16384, 4096], P(('ctx', 'head'))
- grad_key: bfloat16 [16384, 4096], P(('ctx', 'head'))
- grad_value: bfloat16 [16384, 4096], P(('ctx', 'head'))
The draws below stay inside these ranges and needn't reach their ends.
All inputs are finite; a program needn't handle non-finite values.
Results may differ from the reference program's by a relative error of at most 0.0021.
Values may be sent and summed in bfloat16 or wider, within the bound.
A program may use at most 128 MiB of HBM per device.

```python
import jax
import jax.numpy as jnp
from jax import lax

HEADS = 32
HEAD_DIM = 128
SEQ = 16384
GROUP = 128


def block_scale(stream_key, extent, cuts, smallest, high):
    def one(dim, blocks):
        steps = jax.random.uniform(jax.random.fold_in(jax.random.fold_in(stream_key, 6), dim), (blocks,), jnp.float32, smallest / len(cuts), high / len(cuts))
        return jnp.repeat(jnp.exp(steps), extent[dim] // blocks).reshape((-1,) + (1,) * (len(extent) - dim - 1))

    gain = one(*cuts[0])
    for cut in cuts[1:]:
        gain = gain * one(*cut)
    return gain


def normal_values(key, shape, scale, most, cuts=(), held_as=jnp.bfloat16):
    gain = block_scale(key, shape, cuts, -0.22, 0.18) if cuts else 1.0
    drawn = jax.random.normal(key, shape, jnp.float32) * scale * gain
    return jnp.minimum(jnp.maximum(drawn, -most), most).astype(held_as)


def setup_inputs(seed: int = 0) -> dict:
    key_of = jax.random.split(jax.random.key(seed), 5)
    return {
        "queries": normal_values(key_of[0], (SEQ, HEADS * HEAD_DIM), 1.0, 6.0, ((0, 512),)),
        "key_rows": normal_values(key_of[1], (SEQ, HEADS * HEAD_DIM), 1.0, 6.0, ((0, 512),)),
        "value_rows": normal_values(key_of[2], (SEQ, HEADS * HEAD_DIM), 1.0, 6.0, ((0, 512),)),
        "grad_out": normal_values(key_of[3], (SEQ, HEADS * HEAD_DIM), 1.0, 6.0, ((0, 512),)),
    }


def reference(queries, key_rows, value_rows, grad_out):
    blk = GROUP
    count = SEQ // blk
    scale = (HEAD_DIM * SEQ) ** -0.5
    highest = lax.Precision.HIGHEST
    mask = jnp.tril(jnp.ones((blk, blk), jnp.float32))

    def split(array):
        return array.reshape(count, blk, HEADS, HEAD_DIM)

    blocks = (split(queries), split(key_rows), split(value_rows), split(grad_out))

    def prepare(pieces):
        qf, kf, vf, df = [piece.astype(jnp.float32) for piece in pieces]
        scores = (jnp.einsum("thd,shd->hts", qf, kf, precision=highest) * (scale * mask)).astype(jnp.bfloat16)
        dscores = (jnp.einsum("thd,shd->hts", df, vf, precision=highest) * mask).astype(jnp.bfloat16)
        return qf, kf, vf, df, scores.astype(jnp.float32), dscores.astype(jnp.float32)

    def forward_step(kv_state, pieces):
        qf, kf, vf, df, scores, dscores = prepare(pieces)
        grad_q = scale * (jnp.einsum("hts,shd->thd", dscores, kf, precision=highest)
                          + jnp.einsum("tha,hab->thb", df, kv_state, precision=highest))
        kv_state = kv_state + jnp.einsum("tha,thb->hab", vf, kf, precision=highest)
        return kv_state, grad_q.astype(jnp.bfloat16)

    def backward_step(grad_state, pieces):
        qf, kf, vf, df, scores, dscores = prepare(pieces)
        grad_k = scale * (jnp.einsum("hts,thd->shd", dscores, qf, precision=highest)
                          + jnp.einsum("tha,hab->thb", vf, grad_state, precision=highest))
        grad_v = (jnp.einsum("hts,thd->shd", scores, df, precision=highest)
                  + scale * jnp.einsum("thb,hab->tha", kf, grad_state, precision=highest))
        grad_state = grad_state + jnp.einsum("tha,thb->hab", df, qf, precision=highest)
        return grad_state, (grad_k.astype(jnp.bfloat16), grad_v.astype(jnp.bfloat16))

    start = jnp.zeros((HEADS, HEAD_DIM, HEAD_DIM), jnp.float32)
    unused, grad_q = lax.scan(forward_step, start, blocks)
    unused_too, (grad_k, grad_v) = lax.scan(backward_step, start, blocks, reverse=True)
    width = HEADS * HEAD_DIM
    return (grad_q.reshape(SEQ, width), grad_k.reshape(SEQ, width), grad_v.reshape(SEQ, width))
```

```python
import jax
import jax.numpy as jnp
from jax import lax
from jax.sharding import PartitionSpec as P

HEAD_DIM = 128
GROUP = 128


def exclusive_scans(forward_part, backward_part, axis):
    count = lax.axis_size(axis)
    fwd_total, fwd_excl = forward_part, jnp.zeros_like(forward_part)
    bwd_total, bwd_excl = backward_part, jnp.zeros_like(backward_part)
    shift = 1
    while shift < count:
        to_right = [(i, i + shift) for i in range(count - shift)]
        to_left = [(i + shift, i) for i in range(count - shift)]
        got_fwd = lax.ppermute(fwd_total, axis, to_right)
        got_bwd = lax.ppermute(bwd_total, axis, to_left)
        fwd_excl = fwd_excl + got_fwd
        bwd_excl = bwd_excl + got_bwd
        if shift * 2 < count:
            fwd_total = fwd_total + got_fwd
            bwd_total = bwd_total + got_bwd
        shift *= 2
    return fwd_excl, bwd_excl


def per_device(queries, key_rows, value_rows, grad_out):
    stacked = jnp.stack([queries, key_rows, value_rows, grad_out])
    q_all, k_all, v_all, d_all = lax.all_to_all(
        stacked, "head", split_axis=2, concat_axis=1, tiled=True
    )
    rows_here = q_all.shape[0]
    heads_here = q_all.shape[1] // HEAD_DIM
    scale = (HEAD_DIM * rows_here * lax.axis_size("ctx")) ** (-0.5)
    highest = lax.Precision.HIGHEST
    block = GROUP
    nblocks = rows_here // block
    shape_four = (nblocks, block, heads_here, HEAD_DIM)
    q_four = q_all.reshape(shape_four)
    k_four = k_all.reshape(shape_four)
    v_four = v_all.reshape(shape_four)
    d_four = d_all.reshape(shape_four)
    kv_blocks = jnp.einsum("ntha,nthb->nhab", v_four, k_four, preferred_element_type=jnp.float32)
    g_blocks = jnp.einsum("ntha,nthb->nhab", d_four, q_four, preferred_element_type=jnp.float32)
    kv_local = jnp.sum(kv_blocks, axis=0)
    g_local = jnp.sum(g_blocks, axis=0)
    kv_before, g_after = exclusive_scans(kv_local, g_local, "ctx")
    row_ids = lax.broadcasted_iota(jnp.int32, (nblocks, nblocks), 0)
    col_ids = lax.broadcasted_iota(jnp.int32, (nblocks, nblocks), 1)
    strict_lower = (col_ids < row_ids).astype(jnp.float32)
    strict_upper = (col_ids > row_ids).astype(jnp.float32)
    kv_in = kv_before[None] + jnp.einsum(
        "mn,nhab->mhab", strict_lower, kv_blocks, precision=highest
    )
    g_in = g_after[None] + jnp.einsum("mn,nhab->mhab", strict_upper, g_blocks, precision=highest)
    later = lax.broadcasted_iota(jnp.int32, (block, block), 0)
    earlier = lax.broadcasted_iota(jnp.int32, (block, block), 1)
    causal = (later >= earlier).astype(jnp.float32)
    scores = (
        jnp.einsum("nthd,nshd->nhts", q_four, k_four, preferred_element_type=jnp.float32)
        * (scale * causal)
    ).astype(jnp.bfloat16)
    dscores = (
        jnp.einsum("nthd,nshd->nhts", d_four, v_four, preferred_element_type=jnp.float32) * causal
    ).astype(jnp.bfloat16)
    k_float = k_four.astype(jnp.float32)
    v_float = v_four.astype(jnp.float32)
    d_float = d_four.astype(jnp.float32)
    grad_q = scale * (
        jnp.einsum("nhts,nshd->nthd", dscores, k_four, preferred_element_type=jnp.float32)
        + jnp.einsum("ntha,nhab->nthb", d_float, kv_in, precision=highest)
    )
    grad_k = scale * (
        jnp.einsum("nhts,nthd->nshd", dscores, q_four, preferred_element_type=jnp.float32)
        + jnp.einsum("ntha,nhab->nthb", v_float, g_in, precision=highest)
    )
    grad_v = jnp.einsum(
        "nhts,nthd->nshd", scores, d_four, preferred_element_type=jnp.float32
    ) + scale * jnp.einsum("nthb,nhab->ntha", k_float, g_in, precision=highest)
    flat_shape = (rows_here, heads_here * HEAD_DIM)
    grad_q = grad_q.reshape(flat_shape).astype(jnp.bfloat16)
    grad_k = grad_k.reshape(flat_shape).astype(jnp.bfloat16)
    grad_v = grad_v.reshape(flat_shape).astype(jnp.bfloat16)
    grads = jnp.stack([grad_q, grad_k, grad_v])
    result_q, result_k, result_v = lax.all_to_all(
        grads, "head", split_axis=1, concat_axis=2, tiled=True
    )
    return (result_q, result_k, result_v)


def solution(mesh):
    placed = (
        P(("ctx", "head"), None),
        P(("ctx", "head"), None),
        P(("ctx", "head"), None),
        P(("ctx", "head"), None),
    )
    return jax.shard_map(
        per_device,
        mesh=mesh,
        in_specs=placed,
        out_specs=(P(("ctx", "head"), None), P(("ctx", "head"), None), P(("ctx", "head"), None)),
        check_vma=False,
    )
```

```python
import functools

import jax
import jax.numpy as jnp
from jax import lax
from jax.experimental import pallas as pl
from jax.experimental.pallas import tpu as pltpu
from jax.sharding import PartitionSpec as P

HEAD_DIM = 128
GROUP = 128


MESH = pl.DeviceIdType.MESH


def scan_kernel(count, rounds, fwd_in, bwd_in, fwd_out, bwd_out,
                fwd_tot, bwd_tot, fwd_got, bwd_got, send_sems, recv_sems):
    me = lax.axis_index("ctx")
    head = lax.axis_index("head")
    barrier = pltpu.get_barrier_semaphore()
    for k in range(rounds):
        shift = 1 << k

        @pl.when(me + shift < count)
        def _():
            pl.semaphore_signal(barrier, inc=1, device_id=(me + shift, head), device_id_type=MESH)

        @pl.when(me >= shift)
        def _():
            pl.semaphore_signal(barrier, inc=1, device_id=(me - shift, head), device_id_type=MESH)

    peers = 0
    for k in range(rounds):
        shift = 1 << k
        peers = peers + (me + shift < count).astype(jnp.int32) + (me >= shift).astype(jnp.int32)
    pl.semaphore_wait(barrier, peers)

    fwd_out[...] = jnp.zeros_like(fwd_out)
    bwd_out[...] = jnp.zeros_like(bwd_out)

    def copies(k):
        shift = 1 << k
        src_f = fwd_in if k == 0 else fwd_tot.at[k - 1]
        src_b = bwd_in if k == 0 else bwd_tot.at[k - 1]
        to_right = pltpu.make_async_remote_copy(
            src_ref=src_f, dst_ref=fwd_got.at[k], send_sem=send_sems.at[0, k],
            recv_sem=recv_sems.at[0, k], device_id=(me + shift, head), device_id_type=MESH)
        to_left = pltpu.make_async_remote_copy(
            src_ref=src_b, dst_ref=bwd_got.at[k], send_sem=send_sems.at[1, k],
            recv_sem=recv_sems.at[1, k], device_id=(me - shift, head), device_id_type=MESH)
        return src_f, src_b, to_right, to_left

    for k in range(rounds):
        shift = 1 << k
        src_f, src_b, to_right, to_left = copies(k)

        @pl.when(me + shift < count)
        def _():
            to_right.start()

        @pl.when(me >= shift)
        def _():
            to_left.start()

        last = k == rounds - 1

        @pl.when(me >= shift)
        def _():
            to_right.wait_recv()
            got = fwd_got[k]
            fwd_out[...] += got
            if not last:
                fwd_tot[k] = src_f[...] + got

        @pl.when(me < shift)
        def _():
            if not last:
                fwd_tot[k] = src_f[...]

        @pl.when(me + shift < count)
        def _():
            to_left.wait_recv()
            got = bwd_got[k]
            bwd_out[...] += got
            if not last:
                bwd_tot[k] = src_b[...] + got

        @pl.when(me + shift >= count)
        def _():
            if not last:
                bwd_tot[k] = src_b[...]

    for k in range(rounds):
        shift = 1 << k
        src_f, src_b, to_right, to_left = copies(k)

        @pl.when(me + shift < count)
        def _():
            to_right.wait_send()

        @pl.when(me >= shift)
        def _():
            to_left.wait_send()


def exclusive_scans(forward_part, backward_part, axis):
    count = lax.axis_size(axis)
    rounds = max(1, (count - 1).bit_length())
    shape = forward_part.shape
    fwd = forward_part.reshape(-1, shape[-1])
    bwd = backward_part.reshape(-1, shape[-1])
    rows, cols = fwd.shape
    vmem = pl.BlockSpec(memory_space=pltpu.VMEM)
    fwd_excl, bwd_excl = pl.pallas_call(
        functools.partial(scan_kernel, count, rounds),
        out_shape=(jax.ShapeDtypeStruct(fwd.shape, fwd.dtype),) * 2,
        in_specs=[vmem, vmem],
        out_specs=(vmem, vmem),
        scratch_shapes=[
            pltpu.VMEM((rounds, rows, cols), jnp.float32),
            pltpu.VMEM((rounds, rows, cols), jnp.float32),
            pltpu.VMEM((rounds, rows, cols), jnp.float32),
            pltpu.VMEM((rounds, rows, cols), jnp.float32),
            pltpu.SemaphoreType.DMA((2, rounds)),
            pltpu.SemaphoreType.DMA((2, rounds)),
        ],
        compiler_params=pltpu.CompilerParams(collective_id=0, has_side_effects=True,
                                             vmem_limit_bytes=48 * 1024 * 1024),
    )(fwd, bwd)
    return fwd_excl.reshape(shape), bwd_excl.reshape(shape)


def per_device(queries, key_rows, value_rows, grad_out):
    stacked = jnp.stack([queries, key_rows, value_rows, grad_out])
    q_all, k_all, v_all, d_all = lax.all_to_all(
        stacked, "head", split_axis=2, concat_axis=1, tiled=True
    )
    rows_here = q_all.shape[0]
    heads_here = q_all.shape[1] // HEAD_DIM
    scale = (HEAD_DIM * rows_here * lax.axis_size("ctx")) ** (-0.5)
    highest = lax.Precision.HIGHEST
    block = GROUP
    nblocks = rows_here // block
    shape_four = (nblocks, block, heads_here, HEAD_DIM)
    q_four = q_all.reshape(shape_four)
    k_four = k_all.reshape(shape_four)
    v_four = v_all.reshape(shape_four)
    d_four = d_all.reshape(shape_four)
    kv_blocks = jnp.einsum("ntha,nthb->nhab", v_four, k_four, preferred_element_type=jnp.float32)
    g_blocks = jnp.einsum("ntha,nthb->nhab", d_four, q_four, preferred_element_type=jnp.float32)
    kv_local = jnp.sum(kv_blocks, axis=0)
    g_local = jnp.sum(g_blocks, axis=0)
    kv_before, g_after = exclusive_scans(kv_local, g_local, "ctx")
    row_ids = lax.broadcasted_iota(jnp.int32, (nblocks, nblocks), 0)
    col_ids = lax.broadcasted_iota(jnp.int32, (nblocks, nblocks), 1)
    strict_lower = (col_ids < row_ids).astype(jnp.float32)
    strict_upper = (col_ids > row_ids).astype(jnp.float32)
    kv_in = kv_before[None] + jnp.einsum(
        "mn,nhab->mhab", strict_lower, kv_blocks, precision=highest
    )
    g_in = g_after[None] + jnp.einsum("mn,nhab->mhab", strict_upper, g_blocks, precision=highest)
    later = lax.broadcasted_iota(jnp.int32, (block, block), 0)
    earlier = lax.broadcasted_iota(jnp.int32, (block, block), 1)
    causal = (later >= earlier).astype(jnp.float32)
    scores = (
        jnp.einsum("nthd,nshd->nhts", q_four, k_four, preferred_element_type=jnp.float32)
        * (scale * causal)
    ).astype(jnp.bfloat16)
    dscores = (
        jnp.einsum("nthd,nshd->nhts", d_four, v_four, preferred_element_type=jnp.float32) * causal
    ).astype(jnp.bfloat16)
    k_float = k_four.astype(jnp.float32)
    v_float = v_four.astype(jnp.float32)
    d_float = d_four.astype(jnp.float32)
    grad_q = scale * (
        jnp.einsum("nhts,nshd->nthd", dscores, k_four, preferred_element_type=jnp.float32)
        + jnp.einsum("ntha,nhab->nthb", d_float, kv_in, precision=highest)
    )
    grad_k = scale * (
        jnp.einsum("nhts,nthd->nshd", dscores, q_four, preferred_element_type=jnp.float32)
        + jnp.einsum("ntha,nhab->nthb", v_float, g_in, precision=highest)
    )
    grad_v = jnp.einsum(
        "nhts,nthd->nshd", scores, d_four, preferred_element_type=jnp.float32
    ) + scale * jnp.einsum("nthb,nhab->ntha", k_float, g_in, precision=highest)
    flat_shape = (rows_here, heads_here * HEAD_DIM)
    grad_q = grad_q.reshape(flat_shape).astype(jnp.bfloat16)
    grad_k = grad_k.reshape(flat_shape).astype(jnp.bfloat16)
    grad_v = grad_v.reshape(flat_shape).astype(jnp.bfloat16)
    grads = jnp.stack([grad_q, grad_k, grad_v])
    result_q, result_k, result_v = lax.all_to_all(
        grads, "head", split_axis=1, concat_axis=2, tiled=True
    )
    return (result_q, result_k, result_v)


def solution(mesh):
    placed = (
        P(("ctx", "head"), None),
        P(("ctx", "head"), None),
        P(("ctx", "head"), None),
        P(("ctx", "head"), None),
    )
    return jax.shard_map(
        per_device,
        mesh=mesh,
        in_specs=placed,
        out_specs=(P(("ctx", "head"), None), P(("ctx", "head"), None), P(("ctx", "head"), None)),
        check_vma=False,
    )
```

```python
import functools

import jax
import jax.numpy as jnp
from jax import lax
from jax.experimental import pallas as pl
from jax.experimental.pallas import tpu as pltpu
from jax.sharding import PartitionSpec as P

HEAD_DIM = 128
GROUP = 128


MESH = pl.DeviceIdType.MESH


def scan_kernel(count, rounds, fwd_in, bwd_in, fwd_out, bwd_out,
                fwd_tot, bwd_tot, fwd_got, bwd_got, send_sems, recv_sems):
    me = lax.axis_index("ctx")
    head = lax.axis_index("head")
    barrier = pltpu.get_barrier_semaphore()
    for k in range(rounds):
        shift = 1 << k

        @pl.when(me + shift < count)
        def _():
            pl.semaphore_signal(barrier, inc=1, device_id=(me + shift, head), device_id_type=MESH)

        @pl.when(me >= shift)
        def _():
            pl.semaphore_signal(barrier, inc=1, device_id=(me - shift, head), device_id_type=MESH)

    peers = 0
    for k in range(rounds):
        shift = 1 << k
        peers = peers + (me + shift < count).astype(jnp.int32) + (me >= shift).astype(jnp.int32)
    pl.semaphore_wait(barrier, peers)

    fwd_out[...] = jnp.zeros_like(fwd_out)
    bwd_out[...] = jnp.zeros_like(bwd_out)

    def copies(k):
        shift = 1 << k
        src_f = fwd_in if k == 0 else fwd_tot.at[k - 1]
        src_b = bwd_in if k == 0 else bwd_tot.at[k - 1]
        to_right = pltpu.make_async_remote_copy(
            src_ref=src_f, dst_ref=fwd_got.at[k], send_sem=send_sems.at[0, k],
            recv_sem=recv_sems.at[0, k], device_id=(me + shift, head), device_id_type=MESH)
        to_left = pltpu.make_async_remote_copy(
            src_ref=src_b, dst_ref=bwd_got.at[k], send_sem=send_sems.at[1, k],
            recv_sem=recv_sems.at[1, k], device_id=(me - shift, head), device_id_type=MESH)
        return src_f, src_b, to_right, to_left

    for k in range(rounds):
        shift = 1 << k
        src_f, src_b, to_right, to_left = copies(k)

        @pl.when(me + shift < count)
        def _():
            to_right.start()

        @pl.when(me >= shift)
        def _():
            to_left.start()

        last = k == rounds - 1

        @pl.when(me >= shift)
        def _():
            to_right.wait_recv()
            got = fwd_got[k]
            fwd_out[...] += got
            if not last:
                fwd_tot[k] = src_f[...] + got

        @pl.when(me < shift)
        def _():
            if not last:
                fwd_tot[k] = src_f[...]

        @pl.when(me + shift < count)
        def _():
            to_left.wait_recv()
            got = bwd_got[k]
            bwd_out[...] += got
            if not last:
                bwd_tot[k] = src_b[...] + got

        @pl.when(me + shift >= count)
        def _():
            if not last:
                bwd_tot[k] = src_b[...]

    for k in range(rounds):
        shift = 1 << k
        src_f, src_b, to_right, to_left = copies(k)

        @pl.when(me + shift < count)
        def _():
            to_right.wait_send()

        @pl.when(me >= shift)
        def _():
            to_left.wait_send()


def exchange_kernel(count, n_arrays, src_cut, dst_cut, *refs):
    srcs = refs[:n_arrays]
    dsts = refs[n_arrays:2 * n_arrays]
    send_sems, recv_sems, local_sems = refs[2 * n_arrays:]
    me = lax.axis_index("head")
    place = lax.axis_index("ctx")
    barrier = pltpu.get_barrier_semaphore()
    for j in range(count):
        @pl.when(me != j)
        def _():
            pl.semaphore_signal(barrier, inc=1, device_id=(place, j), device_id_type=MESH)
    pl.semaphore_wait(barrier, count - 1)

    def remote(a, j, dst_index):
        return pltpu.make_async_remote_copy(
            src_ref=src_cut(srcs[a], j), dst_ref=dst_cut(dsts[a], dst_index),
            send_sem=send_sems.at[a, j], recv_sem=recv_sems.at[a, me],
            device_id=(place, j), device_id_type=MESH)

    for a in range(n_arrays):
        local = pltpu.make_async_copy(src_cut(srcs[a], me), dst_cut(dsts[a], me), local_sems.at[a])
        local.start()
    for step in range(1, count):
        for a in range(n_arrays):
            j_dyn = lax.rem(me + step, count)
            for j in range(count):
                @pl.when(j_dyn == j)
                def _():
                    remote(a, j, me).start()
    for a in range(n_arrays):
        pltpu.make_async_copy(src_cut(srcs[a], me), dst_cut(dsts[a], me), local_sems.at[a]).wait()
    for a in range(n_arrays):
        for j in range(count):
            @pl.when(me != j)
            def _():
                copy = pltpu.make_async_remote_copy(
                    src_ref=src_cut(srcs[a], j), dst_ref=dst_cut(dsts[a], j),
                    send_sem=send_sems.at[a, j], recv_sem=recv_sems.at[a, j],
                    device_id=(place, j), device_id_type=MESH)
                copy.wait_send()
                copy.wait_recv()


def exchange(arrays, out_shape, src_cut, dst_cut, collective_id):
    count = lax.axis_size("head")
    n_arrays = len(arrays)
    anywhere = pl.BlockSpec(memory_space=pl.ANY)
    return pl.pallas_call(
        functools.partial(exchange_kernel, count, n_arrays, src_cut, dst_cut),
        out_shape=tuple(jax.ShapeDtypeStruct(out_shape, arrays[0].dtype) for _ in arrays),
        in_specs=[anywhere] * n_arrays,
        out_specs=tuple(anywhere for _ in arrays),
        scratch_shapes=[
            pltpu.SemaphoreType.DMA((n_arrays, count)),
            pltpu.SemaphoreType.DMA((n_arrays, count)),
            pltpu.SemaphoreType.DMA((n_arrays,)),
        ],
        compiler_params=pltpu.CompilerParams(collective_id=collective_id, has_side_effects=True),
    )(*arrays)


def exclusive_scans(forward_part, backward_part, axis):
    count = lax.axis_size(axis)
    rounds = max(1, (count - 1).bit_length())
    shape = forward_part.shape
    fwd = forward_part.reshape(-1, shape[-1])
    bwd = backward_part.reshape(-1, shape[-1])
    rows, cols = fwd.shape
    vmem = pl.BlockSpec(memory_space=pltpu.VMEM)
    fwd_excl, bwd_excl = pl.pallas_call(
        functools.partial(scan_kernel, count, rounds),
        out_shape=(jax.ShapeDtypeStruct(fwd.shape, fwd.dtype),) * 2,
        in_specs=[vmem, vmem],
        out_specs=(vmem, vmem),
        scratch_shapes=[
            pltpu.VMEM((rounds, rows, cols), jnp.float32),
            pltpu.VMEM((rounds, rows, cols), jnp.float32),
            pltpu.VMEM((rounds, rows, cols), jnp.float32),
            pltpu.VMEM((rounds, rows, cols), jnp.float32),
            pltpu.SemaphoreType.DMA((2, rounds)),
            pltpu.SemaphoreType.DMA((2, rounds)),
        ],
        compiler_params=pltpu.CompilerParams(collective_id=0, has_side_effects=True,
                                             vmem_limit_bytes=48 * 1024 * 1024),
    )(fwd, bwd)
    return fwd_excl.reshape(shape), bwd_excl.reshape(shape)


def per_device(queries, key_rows, value_rows, grad_out):
    count = lax.axis_size("head")
    rows_in, width = queries.shape
    cols = width // count
    q_all, k_all, v_all, d_all = exchange(
        (queries, key_rows, value_rows, grad_out),
        (rows_in * count, cols),
        lambda ref, j: ref.at[:, pl.ds(j * cols, cols)],
        lambda ref, j: ref.at[pl.ds(j * rows_in, rows_in), :],
        1,
    )
    rows_here = q_all.shape[0]
    heads_here = q_all.shape[1] // HEAD_DIM
    scale = (HEAD_DIM * rows_here * lax.axis_size("ctx")) ** (-0.5)
    highest = lax.Precision.HIGHEST
    block = GROUP
    nblocks = rows_here // block
    shape_four = (nblocks, block, heads_here, HEAD_DIM)
    q_four = q_all.reshape(shape_four)
    k_four = k_all.reshape(shape_four)
    v_four = v_all.reshape(shape_four)
    d_four = d_all.reshape(shape_four)
    kv_blocks = jnp.einsum("ntha,nthb->nhab", v_four, k_four, preferred_element_type=jnp.float32)
    g_blocks = jnp.einsum("ntha,nthb->nhab", d_four, q_four, preferred_element_type=jnp.float32)
    kv_local = jnp.sum(kv_blocks, axis=0)
    g_local = jnp.sum(g_blocks, axis=0)
    kv_before, g_after = exclusive_scans(kv_local, g_local, "ctx")
    row_ids = lax.broadcasted_iota(jnp.int32, (nblocks, nblocks), 0)
    col_ids = lax.broadcasted_iota(jnp.int32, (nblocks, nblocks), 1)
    strict_lower = (col_ids < row_ids).astype(jnp.float32)
    strict_upper = (col_ids > row_ids).astype(jnp.float32)
    kv_in = kv_before[None] + jnp.einsum(
        "mn,nhab->mhab", strict_lower, kv_blocks, precision=highest
    )
    g_in = g_after[None] + jnp.einsum("mn,nhab->mhab", strict_upper, g_blocks, precision=highest)
    later = lax.broadcasted_iota(jnp.int32, (block, block), 0)
    earlier = lax.broadcasted_iota(jnp.int32, (block, block), 1)
    causal = (later >= earlier).astype(jnp.float32)
    scores = (
        jnp.einsum("nthd,nshd->nhts", q_four, k_four, preferred_element_type=jnp.float32)
        * (scale * causal)
    ).astype(jnp.bfloat16)
    dscores = (
        jnp.einsum("nthd,nshd->nhts", d_four, v_four, preferred_element_type=jnp.float32) * causal
    ).astype(jnp.bfloat16)
    k_float = k_four.astype(jnp.float32)
    v_float = v_four.astype(jnp.float32)
    d_float = d_four.astype(jnp.float32)
    grad_q = scale * (
        jnp.einsum("nhts,nshd->nthd", dscores, k_four, preferred_element_type=jnp.float32)
        + jnp.einsum("ntha,nhab->nthb", d_float, kv_in, precision=highest)
    )
    grad_k = scale * (
        jnp.einsum("nhts,nthd->nshd", dscores, q_four, preferred_element_type=jnp.float32)
        + jnp.einsum("ntha,nhab->nthb", v_float, g_in, precision=highest)
    )
    grad_v = jnp.einsum(
        "nhts,nthd->nshd", scores, d_four, preferred_element_type=jnp.float32
    ) + scale * jnp.einsum("nthb,nhab->ntha", k_float, g_in, precision=highest)
    flat_shape = (rows_here, heads_here * HEAD_DIM)
    grad_q = grad_q.reshape(flat_shape).astype(jnp.bfloat16)
    grad_k = grad_k.reshape(flat_shape).astype(jnp.bfloat16)
    grad_v = grad_v.reshape(flat_shape).astype(jnp.bfloat16)
    result_q, result_k, result_v = exchange(
        (grad_q, grad_k, grad_v),
        (rows_in, width),
        lambda ref, j: ref.at[pl.ds(j * rows_in, rows_in), :],
        lambda ref, j: ref.at[:, pl.ds(j * cols, cols)],
        2,
    )
    return (result_q, result_k, result_v)


def solution(mesh):
    placed = (
        P(("ctx", "head"), None),
        P(("ctx", "head"), None),
        P(("ctx", "head"), None),
        P(("ctx", "head"), None),
    )
    return jax.shard_map(
        per_device,
        mesh=mesh,
        in_specs=placed,
        out_specs=(P(("ctx", "head"), None), P(("ctx", "head"), None), P(("ctx", "head"), None)),
        check_vma=False,
    )
```

```python
import functools

import jax
import jax.numpy as jnp
from jax import lax
from jax.experimental import pallas as pl
from jax.experimental.pallas import tpu as pltpu
from jax.sharding import PartitionSpec as P

HEAD_DIM = 128
GROUP = 128


MESH = pl.DeviceIdType.MESH


def scan_kernel(chips, rounds, half, fwd_in, bwd_in, fwd_out, bwd_out,
                peer_f, peer_b, tot_f, tot_b, got_f, got_b, ex_f, ex_b, fin_f, fin_b,
                send_sems, recv_sems):
    me = lax.axis_index("ctx")
    head = lax.axis_index("head")
    core = lax.rem(me, 2)
    chip = me // 2
    partner = me + 1 - 2 * core
    barrier = pltpu.get_barrier_semaphore()
    pl.semaphore_signal(barrier, inc=1, device_id=(partner, head), device_id_type=MESH)
    peers = 1
    for k in range(rounds):
        shift = 1 << k

        @pl.when(chip + shift < chips)
        def _():
            pl.semaphore_signal(barrier, inc=1, device_id=(me + 2 * shift, head), device_id_type=MESH)

        @pl.when(chip >= shift)
        def _():
            pl.semaphore_signal(barrier, inc=1, device_id=(me - 2 * shift, head), device_id_type=MESH)

        peers = peers + (chip + shift < chips).astype(jnp.int32) + (chip >= shift).astype(jnp.int32)
    pl.semaphore_wait(barrier, peers)

    def on_chip(src_f, dst_f, src_b, dst_b, slot):
        return (
            pltpu.make_async_remote_copy(
                src_ref=src_f, dst_ref=dst_f, send_sem=send_sems.at[0, slot],
                recv_sem=recv_sems.at[0, slot], device_id=(partner, head), device_id_type=MESH),
            pltpu.make_async_remote_copy(
                src_ref=src_b, dst_ref=dst_b, send_sem=send_sems.at[1, slot],
                recv_sem=recv_sems.at[1, slot], device_id=(partner, head), device_id_type=MESH),
        )

    first = on_chip(fwd_in, peer_f, bwd_in, peer_b, 0)
    for copy in first:
        copy.start()
    for copy in first:
        copy.wait_recv()

    for mine in range(2):
        rows = pl.ds(mine * half, half)

        @pl.when(core == mine)
        def _():
            tot_f[0] = fwd_in[rows, :] + peer_f[rows, :]
            tot_b[0] = bwd_in[rows, :] + peer_b[rows, :]

    ex_f[...] = jnp.zeros_like(ex_f)
    ex_b[...] = jnp.zeros_like(ex_b)

    def copies(k):
        shift = 1 << k
        to_right = pltpu.make_async_remote_copy(
            src_ref=tot_f.at[k], dst_ref=got_f.at[k], send_sem=send_sems.at[0, k + 1],
            recv_sem=recv_sems.at[0, k + 1], device_id=(me + 2 * shift, head), device_id_type=MESH)
        to_left = pltpu.make_async_remote_copy(
            src_ref=tot_b.at[k], dst_ref=got_b.at[k], send_sem=send_sems.at[1, k + 1],
            recv_sem=recv_sems.at[1, k + 1], device_id=(me - 2 * shift, head), device_id_type=MESH)
        return to_right, to_left

    for k in range(rounds):
        shift = 1 << k
        to_right, to_left = copies(k)
        last = k == rounds - 1

        @pl.when(chip + shift < chips)
        def _():
            to_right.start()

        @pl.when(chip >= shift)
        def _():
            to_left.start()

        @pl.when(chip >= shift)
        def _():
            to_right.wait_recv()
            got = got_f[k]
            ex_f[...] += got
            if not last:
                tot_f[k + 1] = tot_f[k] + got

        @pl.when(chip < shift)
        def _():
            if not last:
                tot_f[k + 1] = tot_f[k]

        @pl.when(chip + shift < chips)
        def _():
            to_left.wait_recv()
            got = got_b[k]
            ex_b[...] += got
            if not last:
                tot_b[k + 1] = tot_b[k] + got

        @pl.when(chip + shift >= chips)
        def _():
            if not last:
                tot_b[k + 1] = tot_b[k]

    last_pair = on_chip(ex_f, fin_f, ex_b, fin_b, rounds + 1)
    for copy in last_pair:
        copy.start()
    for copy in last_pair:
        copy.wait_recv()

    for mine in range(2):
        rows = pl.ds(mine * half, half)
        other = pl.ds((1 - mine) * half, half)

        @pl.when(core == mine)
        def _():
            if mine == 0:
                fwd_out[rows, :] = ex_f[...]
                fwd_out[other, :] = fin_f[...]
                bwd_out[rows, :] = ex_b[...] + peer_b[rows, :]
                bwd_out[other, :] = fin_b[...] + peer_b[other, :]
            else:
                fwd_out[rows, :] = ex_f[...] + peer_f[rows, :]
                fwd_out[other, :] = fin_f[...] + peer_f[other, :]
                bwd_out[rows, :] = ex_b[...]
                bwd_out[other, :] = fin_b[...]

    for copy in first + last_pair:
        copy.wait_send()
    for k in range(rounds):
        shift = 1 << k
        to_right, to_left = copies(k)

        @pl.when(chip + shift < chips)
        def _():
            to_right.wait_send()

        @pl.when(chip >= shift)
        def _():
            to_left.wait_send()


def exclusive_scans(forward_part, backward_part, axis):
    count = lax.axis_size(axis)
    chips = count // 2
    rounds = max(1, (chips - 1).bit_length())
    shape = forward_part.shape
    fwd = forward_part.reshape(-1, shape[-1])
    bwd = backward_part.reshape(-1, shape[-1])
    rows, cols = fwd.shape
    half = rows // 2
    vmem = pl.BlockSpec(memory_space=pltpu.VMEM)
    fwd_excl, bwd_excl = pl.pallas_call(
        functools.partial(scan_kernel, chips, rounds, half),
        out_shape=(jax.ShapeDtypeStruct(fwd.shape, fwd.dtype),) * 2,
        in_specs=[vmem, vmem],
        out_specs=(vmem, vmem),
        scratch_shapes=[
            pltpu.VMEM((rows, cols), jnp.float32),
            pltpu.VMEM((rows, cols), jnp.float32),
            pltpu.VMEM((rounds, half, cols), jnp.float32),
            pltpu.VMEM((rounds, half, cols), jnp.float32),
            pltpu.VMEM((rounds, half, cols), jnp.float32),
            pltpu.VMEM((rounds, half, cols), jnp.float32),
            pltpu.VMEM((half, cols), jnp.float32),
            pltpu.VMEM((half, cols), jnp.float32),
            pltpu.VMEM((half, cols), jnp.float32),
            pltpu.VMEM((half, cols), jnp.float32),
            pltpu.SemaphoreType.DMA((2, rounds + 2)),
            pltpu.SemaphoreType.DMA((2, rounds + 2)),
        ],
        compiler_params=pltpu.CompilerParams(collective_id=0, has_side_effects=True,
                                             vmem_limit_bytes=48 * 1024 * 1024),
    )(fwd, bwd)
    return fwd_excl.reshape(shape), bwd_excl.reshape(shape)


def exchange_kernel(count, n_arrays, src_cut, dst_cut, *refs):
    srcs = refs[:n_arrays]
    dsts = refs[n_arrays:2 * n_arrays]
    send_sems, recv_sems, local_sems = refs[2 * n_arrays:]
    me = lax.axis_index("head")
    place = lax.axis_index("ctx")
    barrier = pltpu.get_barrier_semaphore()
    for j in range(count):
        @pl.when(me != j)
        def _():
            pl.semaphore_signal(barrier, inc=1, device_id=(place, j), device_id_type=MESH)
    pl.semaphore_wait(barrier, count - 1)

    def remote(a, j, dst_index):
        return pltpu.make_async_remote_copy(
            src_ref=src_cut(srcs[a], j), dst_ref=dst_cut(dsts[a], dst_index),
            send_sem=send_sems.at[a, j], recv_sem=recv_sems.at[a, me],
            device_id=(place, j), device_id_type=MESH)

    for a in range(n_arrays):
        local = pltpu.make_async_copy(src_cut(srcs[a], me), dst_cut(dsts[a], me), local_sems.at[a])
        local.start()
    for step in range(1, count):
        for a in range(n_arrays):
            j_dyn = lax.rem(me + step, count)
            for j in range(count):
                @pl.when(j_dyn == j)
                def _():
                    remote(a, j, me).start()
    for a in range(n_arrays):
        pltpu.make_async_copy(src_cut(srcs[a], me), dst_cut(dsts[a], me), local_sems.at[a]).wait()
    for a in range(n_arrays):
        for j in range(count):
            @pl.when(me != j)
            def _():
                copy = pltpu.make_async_remote_copy(
                    src_ref=src_cut(srcs[a], j), dst_ref=dst_cut(dsts[a], j),
                    send_sem=send_sems.at[a, j], recv_sem=recv_sems.at[a, j],
                    device_id=(place, j), device_id_type=MESH)
                copy.wait_send()
                copy.wait_recv()


def exchange(arrays, out_shape, src_cut, dst_cut, collective_id):
    count = lax.axis_size("head")
    n_arrays = len(arrays)
    anywhere = pl.BlockSpec(memory_space=pl.ANY)
    return pl.pallas_call(
        functools.partial(exchange_kernel, count, n_arrays, src_cut, dst_cut),
        out_shape=tuple(jax.ShapeDtypeStruct(out_shape, arrays[0].dtype) for _ in arrays),
        in_specs=[anywhere] * n_arrays,
        out_specs=tuple(anywhere for _ in arrays),
        scratch_shapes=[
            pltpu.SemaphoreType.DMA((n_arrays, count)),
            pltpu.SemaphoreType.DMA((n_arrays, count)),
            pltpu.SemaphoreType.DMA((n_arrays,)),
        ],
        compiler_params=pltpu.CompilerParams(collective_id=collective_id, has_side_effects=True),
    )(*arrays)


def per_device(queries, key_rows, value_rows, grad_out):
    count = lax.axis_size("head")
    rows_in, width = queries.shape
    cols = width // count
    q_all, k_all, v_all, d_all = exchange(
        (queries, key_rows, value_rows, grad_out),
        (rows_in * count, cols),
        lambda ref, j: ref.at[:, pl.ds(j * cols, cols)],
        lambda ref, j: ref.at[pl.ds(j * rows_in, rows_in), :],
        1,
    )
    rows_here = q_all.shape[0]
    heads_here = q_all.shape[1] // HEAD_DIM
    scale = (HEAD_DIM * rows_here * lax.axis_size("ctx")) ** (-0.5)
    highest = lax.Precision.HIGHEST
    block = GROUP
    nblocks = rows_here // block
    shape_four = (nblocks, block, heads_here, HEAD_DIM)
    q_four = q_all.reshape(shape_four)
    k_four = k_all.reshape(shape_four)
    v_four = v_all.reshape(shape_four)
    d_four = d_all.reshape(shape_four)
    kv_blocks = jnp.einsum("ntha,nthb->nhab", v_four, k_four, preferred_element_type=jnp.float32)
    g_blocks = jnp.einsum("ntha,nthb->nhab", d_four, q_four, preferred_element_type=jnp.float32)
    kv_local = jnp.sum(kv_blocks, axis=0)
    g_local = jnp.sum(g_blocks, axis=0)
    kv_before, g_after = exclusive_scans(kv_local, g_local, "ctx")
    row_ids = lax.broadcasted_iota(jnp.int32, (nblocks, nblocks), 0)
    col_ids = lax.broadcasted_iota(jnp.int32, (nblocks, nblocks), 1)
    strict_lower = (col_ids < row_ids).astype(jnp.float32)
    strict_upper = (col_ids > row_ids).astype(jnp.float32)
    kv_in = kv_before[None] + jnp.einsum(
        "mn,nhab->mhab", strict_lower, kv_blocks, precision=highest
    )
    g_in = g_after[None] + jnp.einsum("mn,nhab->mhab", strict_upper, g_blocks, precision=highest)
    later = lax.broadcasted_iota(jnp.int32, (block, block), 0)
    earlier = lax.broadcasted_iota(jnp.int32, (block, block), 1)
    causal = (later >= earlier).astype(jnp.float32)
    scores = (
        jnp.einsum("nthd,nshd->nhts", q_four, k_four, preferred_element_type=jnp.float32)
        * (scale * causal)
    ).astype(jnp.bfloat16)
    dscores = (
        jnp.einsum("nthd,nshd->nhts", d_four, v_four, preferred_element_type=jnp.float32) * causal
    ).astype(jnp.bfloat16)
    k_float = k_four.astype(jnp.float32)
    v_float = v_four.astype(jnp.float32)
    d_float = d_four.astype(jnp.float32)
    grad_q = scale * (
        jnp.einsum("nhts,nshd->nthd", dscores, k_four, preferred_element_type=jnp.float32)
        + jnp.einsum("ntha,nhab->nthb", d_float, kv_in, precision=highest)
    )
    grad_k = scale * (
        jnp.einsum("nhts,nthd->nshd", dscores, q_four, preferred_element_type=jnp.float32)
        + jnp.einsum("ntha,nhab->nthb", v_float, g_in, precision=highest)
    )
    grad_v = jnp.einsum(
        "nhts,nthd->nshd", scores, d_four, preferred_element_type=jnp.float32
    ) + scale * jnp.einsum("nthb,nhab->ntha", k_float, g_in, precision=highest)
    flat_shape = (rows_here, heads_here * HEAD_DIM)
    grad_q = grad_q.reshape(flat_shape).astype(jnp.bfloat16)
    grad_k = grad_k.reshape(flat_shape).astype(jnp.bfloat16)
    grad_v = grad_v.reshape(flat_shape).astype(jnp.bfloat16)
    result_q, result_k, result_v = exchange(
        (grad_q, grad_k, grad_v),
        (rows_in, width),
        lambda ref, j: ref.at[pl.ds(j * rows_in, rows_in), :],
        lambda ref, j: ref.at[:, pl.ds(j * cols, cols)],
        2,
    )
    return (result_q, result_k, result_v)


def solution(mesh):
    placed = (
        P(("ctx", "head"), None),
        P(("ctx", "head"), None),
        P(("ctx", "head"), None),
        P(("ctx", "head"), None),
    )
    return jax.shard_map(
        per_device,
        mesh=mesh,
        in_specs=placed,
        out_specs=(P(("ctx", "head"), None), P(("ctx", "head"), None), P(("ctx", "head"), None)),
        check_vma=False,
    )
```

```python
import functools

import jax
import jax.numpy as jnp
from jax import lax
from jax.experimental import pallas as pl
from jax.experimental.pallas import tpu as pltpu
from jax.sharding import PartitionSpec as P

HEAD_DIM = 128
GROUP = 128


MESH = pl.DeviceIdType.MESH


def _dot(a, b, ta=False, tb=False, precise=False):
    dims = (((0 if ta else 1,), (1 if tb else 0,)), ((), ()))
    return lax.dot_general(a, b, dims, preferred_element_type=jnp.float32,
                           precision=lax.Precision.HIGHEST if precise else None)


def core_kernel(chips, rounds, half, nblocks, heads, scale,
                q_ref, k_ref, v_ref, d_ref, gq_ref, gk_ref, gv_ref,
                fwd_in, bwd_in, kv_blk, g_blk, acc_q, acc_k, acc_v,
                peer_f, peer_b, tot_f, tot_b, got_f, got_b, ex_f, ex_b, fin_f, fin_b,
                fwd_out, bwd_out, send_sems, recv_sems):
    me = lax.axis_index("ctx")
    head = lax.axis_index("head")
    core = lax.rem(me, 2)
    chip = me // 2
    partner = me + 1 - 2 * core
    barrier = pltpu.get_barrier_semaphore()
    pl.semaphore_signal(barrier, inc=1, device_id=(partner, head), device_id_type=MESH)
    peers = 1
    for k in range(rounds):
        shift = 1 << k

        @pl.when(chip + shift < chips)
        def _():
            pl.semaphore_signal(barrier, inc=1, device_id=(me + 2 * shift, head), device_id_type=MESH)

        @pl.when(chip >= shift)
        def _():
            pl.semaphore_signal(barrier, inc=1, device_id=(me - 2 * shift, head), device_id_type=MESH)

        peers = peers + (chip + shift < chips).astype(jnp.int32) + (chip >= shift).astype(jnp.int32)

    blk = GROUP
    dim = HEAD_DIM

    def cut(ref, n, h):
        return ref[n * blk:(n + 1) * blk, h * dim:(h + 1) * dim]

    for h in range(heads):
        rows = slice(h * dim, (h + 1) * dim)
        for n in range(nblocks):
            kv_blk[n, rows, :] = _dot(cut(v_ref, n, h), cut(k_ref, n, h), ta=True)
            g_blk[n, rows, :] = _dot(cut(d_ref, n, h), cut(q_ref, n, h), ta=True)
        kv_sum = kv_blk[0, rows, :]
        g_sum = g_blk[0, rows, :]
        for n in range(1, nblocks):
            kv_sum = kv_sum + kv_blk[n, rows, :]
            g_sum = g_sum + g_blk[n, rows, :]
        fwd_in[rows, :] = kv_sum
        bwd_in[rows, :] = g_sum

    pl.semaphore_wait(barrier, peers)

    def on_chip(src_f, dst_f, src_b, dst_b, slot):
        return (
            pltpu.make_async_remote_copy(
                src_ref=src_f, dst_ref=dst_f, send_sem=send_sems.at[0, slot],
                recv_sem=recv_sems.at[0, slot], device_id=(partner, head), device_id_type=MESH),
            pltpu.make_async_remote_copy(
                src_ref=src_b, dst_ref=dst_b, send_sem=send_sems.at[1, slot],
                recv_sem=recv_sems.at[1, slot], device_id=(partner, head), device_id_type=MESH),
        )

    first = on_chip(fwd_in, peer_f, bwd_in, peer_b, 0)
    for copy in first:
        copy.start()

    later = lax.broadcasted_iota(jnp.int32, (blk, blk), 0)
    earlier = lax.broadcasted_iota(jnp.int32, (blk, blk), 1)
    causal = later >= earlier
    for h in range(heads):
        for n in range(nblocks):
            qb, kb, vb, db = (cut(r, n, h) for r in (q_ref, k_ref, v_ref, d_ref))
            scores = jnp.where(causal, _dot(qb, kb, tb=True) * scale, 0.0).astype(jnp.bfloat16)
            dscores = jnp.where(causal, _dot(db, vb, tb=True), 0.0).astype(jnp.bfloat16)
            out_rows = slice(n * blk, (n + 1) * blk)
            out_cols = slice(h * dim, (h + 1) * dim)
            acc_q[out_rows, out_cols] = _dot(dscores, kb)
            acc_k[out_rows, out_cols] = _dot(dscores, qb, ta=True)
            acc_v[out_rows, out_cols] = _dot(scores, db, ta=True)

    for copy in first:
        copy.wait_recv()

    for mine in range(2):
        rows = pl.ds(mine * half, half)

        @pl.when(core == mine)
        def _():
            tot_f[0] = fwd_in[rows, :] + peer_f[rows, :]
            tot_b[0] = bwd_in[rows, :] + peer_b[rows, :]

    ex_f[...] = jnp.zeros_like(ex_f)
    ex_b[...] = jnp.zeros_like(ex_b)

    def copies(k):
        shift = 1 << k
        to_right = pltpu.make_async_remote_copy(
            src_ref=tot_f.at[k], dst_ref=got_f.at[k], send_sem=send_sems.at[0, k + 1],
            recv_sem=recv_sems.at[0, k + 1], device_id=(me + 2 * shift, head), device_id_type=MESH)
        to_left = pltpu.make_async_remote_copy(
            src_ref=tot_b.at[k], dst_ref=got_b.at[k], send_sem=send_sems.at[1, k + 1],
            recv_sem=recv_sems.at[1, k + 1], device_id=(me - 2 * shift, head), device_id_type=MESH)
        return to_right, to_left

    for k in range(rounds):
        shift = 1 << k
        to_right, to_left = copies(k)
        last = k == rounds - 1

        @pl.when(chip + shift < chips)
        def _():
            to_right.start()

        @pl.when(chip >= shift)
        def _():
            to_left.start()

        @pl.when(chip >= shift)
        def _():
            to_right.wait_recv()
            got = got_f[k]
            ex_f[...] += got
            if not last:
                tot_f[k + 1] = tot_f[k] + got

        @pl.when(chip < shift)
        def _():
            if not last:
                tot_f[k + 1] = tot_f[k]

        @pl.when(chip + shift < chips)
        def _():
            to_left.wait_recv()
            got = got_b[k]
            ex_b[...] += got
            if not last:
                tot_b[k + 1] = tot_b[k] + got

        @pl.when(chip + shift >= chips)
        def _():
            if not last:
                tot_b[k + 1] = tot_b[k]

    last_pair = on_chip(ex_f, fin_f, ex_b, fin_b, rounds + 1)
    for copy in last_pair:
        copy.start()
    for copy in last_pair:
        copy.wait_recv()

    for mine in range(2):
        rows = pl.ds(mine * half, half)
        other = pl.ds((1 - mine) * half, half)

        @pl.when(core == mine)
        def _():
            if mine == 0:
                fwd_out[rows, :] = ex_f[...]
                fwd_out[other, :] = fin_f[...]
                bwd_out[rows, :] = ex_b[...] + peer_b[rows, :]
                bwd_out[other, :] = fin_b[...] + peer_b[other, :]
            else:
                fwd_out[rows, :] = ex_f[...] + peer_f[rows, :]
                fwd_out[other, :] = fin_f[...] + peer_f[other, :]
                bwd_out[rows, :] = ex_b[...]
                bwd_out[other, :] = fin_b[...]

    for h in range(heads):
        rows = slice(h * dim, (h + 1) * dim)
        kv_in = fwd_out[rows, :]
        kv_states = []
        for n in range(nblocks):
            kv_states.append(kv_in)
            if n + 1 < nblocks:
                kv_in = kv_in + kv_blk[n, rows, :]
        g_in = bwd_out[rows, :]
        g_states = [None] * nblocks
        for n in reversed(range(nblocks)):
            g_states[n] = g_in
            if n > 0:
                g_in = g_in + g_blk[n, rows, :]
        for n in range(nblocks):
            out_rows = slice(n * blk, (n + 1) * blk)
            out_cols = slice(h * dim, (h + 1) * dim)
            kf = cut(k_ref, n, h).astype(jnp.float32)
            vf = cut(v_ref, n, h).astype(jnp.float32)
            df = cut(d_ref, n, h).astype(jnp.float32)
            kv_s = kv_states[n]
            g_s = g_states[n]
            gq_ref[out_rows, out_cols] = (
                scale * (acc_q[out_rows, out_cols] + _dot(df, kv_s, precise=True))
            ).astype(gq_ref.dtype)
            gk_ref[out_rows, out_cols] = (
                scale * (acc_k[out_rows, out_cols] + _dot(vf, g_s, precise=True))
            ).astype(gk_ref.dtype)
            gv_ref[out_rows, out_cols] = (
                acc_v[out_rows, out_cols] + scale * _dot(kf, g_s, tb=True, precise=True)
            ).astype(gv_ref.dtype)

    for copy in first + last_pair:
        copy.wait_send()
    for k in range(rounds):
        shift = 1 << k
        to_right, to_left = copies(k)

        @pl.when(chip + shift < chips)
        def _():
            to_right.wait_send()

        @pl.when(chip >= shift)
        def _():
            to_left.wait_send()


def core_math(q_all, k_all, v_all, d_all, scale):
    count = lax.axis_size("ctx")
    chips = count // 2
    rounds = max(1, (chips - 1).bit_length())
    tokens, width = q_all.shape
    heads = width // HEAD_DIM
    nblocks = tokens // GROUP
    rows = heads * HEAD_DIM
    half = rows // 2
    cols = HEAD_DIM
    vmem = pl.BlockSpec(memory_space=pltpu.VMEM)
    f32 = jnp.float32
    return pl.pallas_call(
        functools.partial(core_kernel, chips, rounds, half, nblocks, heads, scale),
        out_shape=(jax.ShapeDtypeStruct(q_all.shape, q_all.dtype),) * 3,
        in_specs=[vmem] * 4,
        out_specs=(vmem,) * 3,
        scratch_shapes=[
            pltpu.VMEM((rows, cols), f32),
            pltpu.VMEM((rows, cols), f32),
            pltpu.VMEM((nblocks, rows, cols), f32),
            pltpu.VMEM((nblocks, rows, cols), f32),
            pltpu.VMEM((tokens, width), f32),
            pltpu.VMEM((tokens, width), f32),
            pltpu.VMEM((tokens, width), f32),
            pltpu.VMEM((rows, cols), f32),
            pltpu.VMEM((rows, cols), f32),
            pltpu.VMEM((rounds, half, cols), f32),
            pltpu.VMEM((rounds, half, cols), f32),
            pltpu.VMEM((rounds, half, cols), f32),
            pltpu.VMEM((rounds, half, cols), f32),
            pltpu.VMEM((half, cols), f32),
            pltpu.VMEM((half, cols), f32),
            pltpu.VMEM((half, cols), f32),
            pltpu.VMEM((half, cols), f32),
            pltpu.VMEM((rows, cols), f32),
            pltpu.VMEM((rows, cols), f32),
            pltpu.SemaphoreType.DMA((2, rounds + 2)),
            pltpu.SemaphoreType.DMA((2, rounds + 2)),
        ],
        compiler_params=pltpu.CompilerParams(collective_id=0, has_side_effects=True,
                                             vmem_limit_bytes=48 * 1024 * 1024),
    )(q_all, k_all, v_all, d_all)


def exchange_kernel(count, n_arrays, src_cut, dst_cut, *refs):
    srcs = refs[:n_arrays]
    dsts = refs[n_arrays:2 * n_arrays]
    send_sems, recv_sems, local_sems = refs[2 * n_arrays:]
    me = lax.axis_index("head")
    place = lax.axis_index("ctx")
    barrier = pltpu.get_barrier_semaphore()
    for j in range(count):
        @pl.when(me != j)
        def _():
            pl.semaphore_signal(barrier, inc=1, device_id=(place, j), device_id_type=MESH)
    pl.semaphore_wait(barrier, count - 1)

    def remote(a, j, dst_index):
        return pltpu.make_async_remote_copy(
            src_ref=src_cut(srcs[a], j), dst_ref=dst_cut(dsts[a], dst_index),
            send_sem=send_sems.at[a, j], recv_sem=recv_sems.at[a, me],
            device_id=(place, j), device_id_type=MESH)

    for a in range(n_arrays):
        local = pltpu.make_async_copy(src_cut(srcs[a], me), dst_cut(dsts[a], me), local_sems.at[a])
        local.start()
    for step in range(1, count):
        for a in range(n_arrays):
            j_dyn = lax.rem(me + step, count)
            for j in range(count):
                @pl.when(j_dyn == j)
                def _():
                    remote(a, j, me).start()
    for a in range(n_arrays):
        pltpu.make_async_copy(src_cut(srcs[a], me), dst_cut(dsts[a], me), local_sems.at[a]).wait()
    for a in range(n_arrays):
        for j in range(count):
            @pl.when(me != j)
            def _():
                copy = pltpu.make_async_remote_copy(
                    src_ref=src_cut(srcs[a], j), dst_ref=dst_cut(dsts[a], j),
                    send_sem=send_sems.at[a, j], recv_sem=recv_sems.at[a, j],
                    device_id=(place, j), device_id_type=MESH)
                copy.wait_send()
                copy.wait_recv()


def exchange(arrays, out_shape, src_cut, dst_cut, collective_id):
    count = lax.axis_size("head")
    n_arrays = len(arrays)
    anywhere = pl.BlockSpec(memory_space=pl.ANY)
    return pl.pallas_call(
        functools.partial(exchange_kernel, count, n_arrays, src_cut, dst_cut),
        out_shape=tuple(jax.ShapeDtypeStruct(out_shape, arrays[0].dtype) for _ in arrays),
        in_specs=[anywhere] * n_arrays,
        out_specs=tuple(anywhere for _ in arrays),
        scratch_shapes=[
            pltpu.SemaphoreType.DMA((n_arrays, count)),
            pltpu.SemaphoreType.DMA((n_arrays, count)),
            pltpu.SemaphoreType.DMA((n_arrays,)),
        ],
        compiler_params=pltpu.CompilerParams(collective_id=collective_id, has_side_effects=True),
    )(*arrays)


def per_device(queries, key_rows, value_rows, grad_out):
    count = lax.axis_size("head")
    rows_in, width = queries.shape
    cols = width // count
    q_all, k_all, v_all, d_all = exchange(
        (queries, key_rows, value_rows, grad_out),
        (rows_in * count, cols),
        lambda ref, j: ref.at[:, pl.ds(j * cols, cols)],
        lambda ref, j: ref.at[pl.ds(j * rows_in, rows_in), :],
        1,
    )
    rows_here = q_all.shape[0]
    scale = (HEAD_DIM * rows_here * lax.axis_size("ctx")) ** (-0.5)
    grad_q, grad_k, grad_v = core_math(q_all, k_all, v_all, d_all, scale)
    result_q, result_k, result_v = exchange(
        (grad_q, grad_k, grad_v),
        (rows_in, width),
        lambda ref, j: ref.at[pl.ds(j * rows_in, rows_in), :],
        lambda ref, j: ref.at[:, pl.ds(j * cols, cols)],
        2,
    )
    return (result_q, result_k, result_v)


def solution(mesh):
    placed = (
        P(("ctx", "head"), None),
        P(("ctx", "head"), None),
        P(("ctx", "head"), None),
        P(("ctx", "head"), None),
    )
    return jax.shard_map(
        per_device,
        mesh=mesh,
        in_specs=placed,
        out_specs=(P(("ctx", "head"), None), P(("ctx", "head"), None), P(("ctx", "head"), None)),
        check_vma=False,
    )
```

```python
import functools

import jax
import jax.numpy as jnp
from jax import lax
from jax.experimental import pallas as pl
from jax.experimental.pallas import tpu as pltpu
from jax.sharding import PartitionSpec as P

HEAD_DIM = 128
GROUP = 128


MESH = pl.DeviceIdType.MESH


def _dot(a, b, ta=False, tb=False, precise=False):
    dims = (((0 if ta else 1,), (1 if tb else 0,)), ((), ()))
    return lax.dot_general(a, b, dims, preferred_element_type=jnp.float32,
                           precision=lax.Precision.HIGHEST if precise else None)


def core_kernel(plane, planes, rounds, half, nblocks, heads, scale,
                q_ref, k_ref, v_ref, d_ref, gq_ref, gk_ref, gv_ref,
                fwd_in, bwd_in, kv_blk, g_blk, acc_q, acc_k, acc_v,
                peer_f, peer_b, th_f, th_b, in_b1, pre, tz_f, tz_b, got_f, got_b,
                ez_f, ez_b, out_d, in_d, res_f, res_b, fin_f, fin_b,
                fwd_out, bwd_out, sems):
    me = lax.axis_index("ctx")
    head = lax.axis_index("head")
    core = lax.rem(me, 2)
    chip = me // 2
    x = lax.rem(chip, plane)
    z = chip // plane
    partner = me + 1 - 2 * core
    qr = half // plane

    def dev(xp, zp):
        return ((zp * plane + xp) * 2 + core, head)

    barrier = pltpu.get_barrier_semaphore()
    pl.semaphore_signal(barrier, inc=1, device_id=(partner, head), device_id_type=MESH)
    peers = 1
    for xp in range(plane):
        @pl.when(x != xp)
        def _():
            pl.semaphore_signal(barrier, inc=1, device_id=dev(xp, z), device_id_type=MESH)

        peers = peers + (x != xp).astype(jnp.int32)
    for k in range(rounds):
        shift = 1 << k

        @pl.when(z + shift < planes)
        def _():
            pl.semaphore_signal(barrier, inc=1, device_id=dev(x, z + shift), device_id_type=MESH)

        @pl.when(z >= shift)
        def _():
            pl.semaphore_signal(barrier, inc=1, device_id=dev(x, z - shift), device_id_type=MESH)

        peers = peers + (z + shift < planes).astype(jnp.int32) + (z >= shift).astype(jnp.int32)

    blk = GROUP
    dim = HEAD_DIM

    def cut(ref, n, h):
        return ref[n * blk:(n + 1) * blk, h * dim:(h + 1) * dim]

    for h in range(heads):
        rows = slice(h * dim, (h + 1) * dim)
        for n in range(nblocks):
            kv_blk[n, rows, :] = _dot(cut(v_ref, n, h), cut(k_ref, n, h), ta=True)
            g_blk[n, rows, :] = _dot(cut(d_ref, n, h), cut(q_ref, n, h), ta=True)
        kv_sum = kv_blk[0, rows, :]
        g_sum = g_blk[0, rows, :]
        for n in range(1, nblocks):
            kv_sum = kv_sum + kv_blk[n, rows, :]
            g_sum = g_sum + g_blk[n, rows, :]
        fwd_in[rows, :] = kv_sum
        bwd_in[rows, :] = g_sum

    pl.semaphore_wait(barrier, peers)

    def remote(src, dst, sem_send, sem_recv, device):
        return pltpu.make_async_remote_copy(
            src_ref=src, dst_ref=dst, send_sem=sem_send, recv_sem=sem_recv,
            device_id=device, device_id_type=MESH)

    first = (remote(fwd_in, peer_f, sems.at[0, 0, 0, 0], sems.at[1, 0, 0, 0], (partner, head)),
             remote(bwd_in, peer_b, sems.at[0, 0, 1, 0], sems.at[1, 0, 1, 0], (partner, head)))
    for copy in first:
        copy.start()

    later = lax.broadcasted_iota(jnp.int32, (blk, blk), 0)
    earlier = lax.broadcasted_iota(jnp.int32, (blk, blk), 1)
    causal = later >= earlier
    for h in range(heads):
        for n in range(nblocks):
            qb, kb, vb, db = (cut(r, n, h) for r in (q_ref, k_ref, v_ref, d_ref))
            scores = jnp.where(causal, _dot(qb, kb, tb=True) * scale, 0.0).astype(jnp.bfloat16)
            dscores = jnp.where(causal, _dot(db, vb, tb=True), 0.0).astype(jnp.bfloat16)
            out_rows = slice(n * blk, (n + 1) * blk)
            out_cols = slice(h * dim, (h + 1) * dim)
            acc_q[out_rows, out_cols] = _dot(dscores, kb)
            acc_k[out_rows, out_cols] = _dot(dscores, qb, ta=True)
            acc_v[out_rows, out_cols] = _dot(scores, db, ta=True)

    for copy in first:
        copy.wait_recv()

    for mine in range(2):
        rows = pl.ds(mine * half, half)

        @pl.when(core == mine)
        def _():
            th_f[...] = fwd_in[rows, :] + peer_f[rows, :]
            th_b[...] = bwd_in[rows, :] + peer_b[rows, :]

    halves = (th_f, th_b)

    def scatter(s, xp):
        return remote(halves[s].at[pl.ds(xp * qr, qr)], in_b1.at[s, x],
                      sems.at[0, 2, s, xp], sems.at[1, 2, s, x], dev(xp, z))

    def scatter_in(s, xp):
        return remote(halves[s].at[pl.ds(xp * qr, qr)], in_b1.at[s, xp],
                      sems.at[0, 2, s, xp], sems.at[1, 2, s, xp], dev(xp, z))

    for s in range(2):
        for xp in range(plane):
            @pl.when(x != xp)
            def _():
                scatter(s, xp).start()
    for s in range(2):
        in_b1[s, x] = halves[s][pl.ds(x * qr, qr), :]
    for s in range(2):
        for xp in range(plane):
            @pl.when(x != xp)
            def _():
                scatter_in(s, xp).wait_recv()

    run = jnp.zeros((qr, HEAD_DIM), jnp.float32)
    for xp in range(plane):
        pre[0, xp] = run
        run = run + in_b1[0, xp]
    tz_f[0] = run
    run = jnp.zeros((qr, HEAD_DIM), jnp.float32)
    for xp in reversed(range(plane)):
        pre[1, xp] = run
        run = run + in_b1[1, xp]
    tz_b[0] = run

    ez_f[...] = jnp.zeros_like(ez_f)
    ez_b[...] = jnp.zeros_like(ez_b)

    def z_copies(k):
        shift = 1 << k
        up = remote(tz_f.at[k], got_f.at[k], sems.at[0, 3, 0, k], sems.at[1, 3, 0, k], dev(x, z + shift))
        down = remote(tz_b.at[k], got_b.at[k], sems.at[0, 3, 1, k], sems.at[1, 3, 1, k], dev(x, z - shift))
        return up, down

    for k in range(rounds):
        shift = 1 << k
        up, down = z_copies(k)
        last = k == rounds - 1

        @pl.when(z + shift < planes)
        def _():
            up.start()

        @pl.when(z >= shift)
        def _():
            down.start()

        @pl.when(z >= shift)
        def _():
            up.wait_recv()
            got = got_f[k]
            ez_f[...] += got
            if not last:
                tz_f[k + 1] = tz_f[k] + got

        @pl.when(z < shift)
        def _():
            if not last:
                tz_f[k + 1] = tz_f[k]

        @pl.when(z + shift < planes)
        def _():
            down.wait_recv()
            got = got_b[k]
            ez_b[...] += got
            if not last:
                tz_b[k + 1] = tz_b[k] + got

        @pl.when(z + shift >= planes)
        def _():
            if not last:
                tz_b[k + 1] = tz_b[k]

    zs = (ez_f, ez_b)
    for s in range(2):
        for xp in range(plane):
            out_d[s, xp] = zs[s][...] + pre[s, xp]

    def gather(s, xp):
        return remote(out_d.at[s, xp], in_d.at[s, x],
                      sems.at[0, 4, s, xp], sems.at[1, 4, s, x], dev(xp, z))

    def gather_in(s, xp):
        return remote(out_d.at[s, xp], in_d.at[s, xp],
                      sems.at[0, 4, s, xp], sems.at[1, 4, s, xp], dev(xp, z))

    for s in range(2):
        for xp in range(plane):
            @pl.when(x != xp)
            def _():
                gather(s, xp).start()
    results = (res_f, res_b)
    for s in range(2):
        results[s][pl.ds(x * qr, qr), :] = out_d[s, x]
    for s in range(2):
        for xp in range(plane):
            @pl.when(x != xp)
            def _():
                gather_in(s, xp).wait_recv()
                results[s][xp * qr:(xp + 1) * qr, :] = in_d[s, xp]

    last_pair = (remote(res_f, fin_f, sems.at[0, 1, 0, 0], sems.at[1, 1, 0, 0], (partner, head)),
                 remote(res_b, fin_b, sems.at[0, 1, 1, 0], sems.at[1, 1, 1, 0], (partner, head)))
    for copy in last_pair:
        copy.start()
    for copy in last_pair:
        copy.wait_recv()

    for mine in range(2):
        rows = pl.ds(mine * half, half)
        other = pl.ds((1 - mine) * half, half)

        @pl.when(core == mine)
        def _():
            if mine == 0:
                fwd_out[rows, :] = res_f[...]
                fwd_out[other, :] = fin_f[...]
                bwd_out[rows, :] = res_b[...] + peer_b[rows, :]
                bwd_out[other, :] = fin_b[...] + peer_b[other, :]
            else:
                fwd_out[rows, :] = res_f[...] + peer_f[rows, :]
                fwd_out[other, :] = fin_f[...] + peer_f[other, :]
                bwd_out[rows, :] = res_b[...]
                bwd_out[other, :] = fin_b[...]

    for h in range(heads):
        rows = slice(h * dim, (h + 1) * dim)
        kv_in = fwd_out[rows, :]
        kv_states = []
        for n in range(nblocks):
            kv_states.append(kv_in)
            if n + 1 < nblocks:
                kv_in = kv_in + kv_blk[n, rows, :]
        g_in = bwd_out[rows, :]
        g_states = [None] * nblocks
        for n in reversed(range(nblocks)):
            g_states[n] = g_in
            if n > 0:
                g_in = g_in + g_blk[n, rows, :]
        for n in range(nblocks):
            out_rows = slice(n * blk, (n + 1) * blk)
            out_cols = slice(h * dim, (h + 1) * dim)
            kf = cut(k_ref, n, h).astype(jnp.float32)
            vf = cut(v_ref, n, h).astype(jnp.float32)
            df = cut(d_ref, n, h).astype(jnp.float32)
            kv_s = kv_states[n]
            g_s = g_states[n]
            gq_ref[out_rows, out_cols] = (
                scale * (acc_q[out_rows, out_cols] + _dot(df, kv_s, precise=True))
            ).astype(gq_ref.dtype)
            gk_ref[out_rows, out_cols] = (
                scale * (acc_k[out_rows, out_cols] + _dot(vf, g_s, precise=True))
            ).astype(gk_ref.dtype)
            gv_ref[out_rows, out_cols] = (
                acc_v[out_rows, out_cols] + scale * _dot(kf, g_s, tb=True, precise=True)
            ).astype(gv_ref.dtype)

    for copy in first + last_pair:
        copy.wait_send()
    for s in range(2):
        for xp in range(plane):
            @pl.when(x != xp)
            def _():
                scatter(s, xp).wait_send()
                gather(s, xp).wait_send()
    for k in range(rounds):
        shift = 1 << k
        up, down = z_copies(k)

        @pl.when(z + shift < planes)
        def _():
            up.wait_send()

        @pl.when(z >= shift)
        def _():
            down.wait_send()


PLANE = 4


def core_math(q_all, k_all, v_all, d_all, scale):
    count = lax.axis_size("ctx")
    chips = count // 2
    plane = PLANE if chips % PLANE == 0 else 1
    planes = chips // plane
    rounds = max(1, (planes - 1).bit_length())
    tokens, width = q_all.shape
    heads = width // HEAD_DIM
    nblocks = tokens // GROUP
    rows = heads * HEAD_DIM
    half = rows // 2
    qr = half // plane
    cols = HEAD_DIM
    vmem = pl.BlockSpec(memory_space=pltpu.VMEM)
    f32 = jnp.float32
    return pl.pallas_call(
        functools.partial(core_kernel, plane, planes, rounds, half, nblocks, heads, scale),
        out_shape=(jax.ShapeDtypeStruct(q_all.shape, q_all.dtype),) * 3,
        in_specs=[vmem] * 4,
        out_specs=(vmem,) * 3,
        scratch_shapes=[
            pltpu.VMEM((rows, cols), f32),
            pltpu.VMEM((rows, cols), f32),
            pltpu.VMEM((nblocks, rows, cols), f32),
            pltpu.VMEM((nblocks, rows, cols), f32),
            pltpu.VMEM((tokens, width), f32),
            pltpu.VMEM((tokens, width), f32),
            pltpu.VMEM((tokens, width), f32),
            pltpu.VMEM((rows, cols), f32),
            pltpu.VMEM((rows, cols), f32),
            pltpu.VMEM((half, cols), f32),
            pltpu.VMEM((half, cols), f32),
            pltpu.VMEM((2, plane, qr, cols), f32),
            pltpu.VMEM((2, plane, qr, cols), f32),
            pltpu.VMEM((rounds, qr, cols), f32),
            pltpu.VMEM((rounds, qr, cols), f32),
            pltpu.VMEM((rounds, qr, cols), f32),
            pltpu.VMEM((rounds, qr, cols), f32),
            pltpu.VMEM((qr, cols), f32),
            pltpu.VMEM((qr, cols), f32),
            pltpu.VMEM((2, plane, qr, cols), f32),
            pltpu.VMEM((2, plane, qr, cols), f32),
            pltpu.VMEM((half, cols), f32),
            pltpu.VMEM((half, cols), f32),
            pltpu.VMEM((half, cols), f32),
            pltpu.VMEM((half, cols), f32),
            pltpu.VMEM((rows, cols), f32),
            pltpu.VMEM((rows, cols), f32),
            pltpu.SemaphoreType.DMA((2, 5, 2, max(plane, rounds))),
        ],
        compiler_params=pltpu.CompilerParams(collective_id=0, has_side_effects=True,
                                             vmem_limit_bytes=48 * 1024 * 1024),
    )(q_all, k_all, v_all, d_all)


def exchange_kernel(count, n_arrays, src_cut, dst_cut, *refs):
    srcs = refs[:n_arrays]
    dsts = refs[n_arrays:2 * n_arrays]
    send_sems, recv_sems, local_sems = refs[2 * n_arrays:]
    me = lax.axis_index("head")
    place = lax.axis_index("ctx")
    barrier = pltpu.get_barrier_semaphore()
    for j in range(count):
        @pl.when(me != j)
        def _():
            pl.semaphore_signal(barrier, inc=1, device_id=(place, j), device_id_type=MESH)
    pl.semaphore_wait(barrier, count - 1)

    def remote(a, j, dst_index):
        return pltpu.make_async_remote_copy(
            src_ref=src_cut(srcs[a], j), dst_ref=dst_cut(dsts[a], dst_index),
            send_sem=send_sems.at[a, j], recv_sem=recv_sems.at[a, me],
            device_id=(place, j), device_id_type=MESH)

    for a in range(n_arrays):
        local = pltpu.make_async_copy(src_cut(srcs[a], me), dst_cut(dsts[a], me), local_sems.at[a])
        local.start()
    for step in range(1, count):
        for a in range(n_arrays):
            j_dyn = lax.rem(me + step, count)
            for j in range(count):
                @pl.when(j_dyn == j)
                def _():
                    remote(a, j, me).start()
    for a in range(n_arrays):
        pltpu.make_async_copy(src_cut(srcs[a], me), dst_cut(dsts[a], me), local_sems.at[a]).wait()
    for a in range(n_arrays):
        for j in range(count):
            @pl.when(me != j)
            def _():
                copy = pltpu.make_async_remote_copy(
                    src_ref=src_cut(srcs[a], j), dst_ref=dst_cut(dsts[a], j),
                    send_sem=send_sems.at[a, j], recv_sem=recv_sems.at[a, j],
                    device_id=(place, j), device_id_type=MESH)
                copy.wait_send()
                copy.wait_recv()


def exchange(arrays, out_shape, src_cut, dst_cut, collective_id):
    count = lax.axis_size("head")
    if count == 1:
        return tuple(arrays)
    n_arrays = len(arrays)
    anywhere = pl.BlockSpec(memory_space=pl.ANY)
    return pl.pallas_call(
        functools.partial(exchange_kernel, count, n_arrays, src_cut, dst_cut),
        out_shape=tuple(jax.ShapeDtypeStruct(out_shape, arrays[0].dtype) for _ in arrays),
        in_specs=[anywhere] * n_arrays,
        out_specs=tuple(anywhere for _ in arrays),
        scratch_shapes=[
            pltpu.SemaphoreType.DMA((n_arrays, count)),
            pltpu.SemaphoreType.DMA((n_arrays, count)),
            pltpu.SemaphoreType.DMA((n_arrays,)),
        ],
        compiler_params=pltpu.CompilerParams(collective_id=collective_id, has_side_effects=True),
    )(*arrays)


def per_device(queries, key_rows, value_rows, grad_out):
    count = lax.axis_size("head")
    rows_in, width = queries.shape
    cols = width // count
    q_all, k_all, v_all, d_all = exchange(
        (queries, key_rows, value_rows, grad_out),
        (rows_in * count, cols),
        lambda ref, j: ref.at[:, pl.ds(j * cols, cols)],
        lambda ref, j: ref.at[pl.ds(j * rows_in, rows_in), :],
        1,
    )
    rows_here = q_all.shape[0]
    scale = (HEAD_DIM * rows_here * lax.axis_size("ctx")) ** (-0.5)
    grad_q, grad_k, grad_v = core_math(q_all, k_all, v_all, d_all, scale)
    result_q, result_k, result_v = exchange(
        (grad_q, grad_k, grad_v),
        (rows_in, width),
        lambda ref, j: ref.at[pl.ds(j * rows_in, rows_in), :],
        lambda ref, j: ref.at[:, pl.ds(j * cols, cols)],
        2,
    )
    return (result_q, result_k, result_v)


def solution(mesh):
    placed = (
        P(("ctx", "head"), None),
        P(("ctx", "head"), None),
        P(("ctx", "head"), None),
        P(("ctx", "head"), None),
    )
    return jax.shard_map(
        per_device,
        mesh=mesh,
        in_specs=placed,
        out_specs=(P(("ctx", "head"), None), P(("ctx", "head"), None), P(("ctx", "head"), None)),
        check_vma=False,
    )
```

```python
import functools

import jax
import jax.numpy as jnp
from jax import lax
from jax.experimental import pallas as pl
from jax.experimental.pallas import tpu as pltpu
from jax.sharding import PartitionSpec as P

HEAD_DIM = 128
GROUP = 128


MESH = pl.DeviceIdType.MESH


def _dot(a, b, ta=False, tb=False, precise=False):
    dims = (((0 if ta else 1,), (1 if tb else 0,)), ((), ()))
    return lax.dot_general(a, b, dims, preferred_element_type=jnp.float32,
                           precision=lax.Precision.HIGHEST if precise else None)


def core_kernel(plane, planes, rounds, half, nblocks, heads, scale,
                q_hbm, k_hbm, v_hbm, d_hbm, gq_hbm, gk_hbm, gv_hbm,
                q_ref, k_ref, v_ref, d_ref, gq_ref, gk_ref, gv_ref, io_sems,
                fwd_in, bwd_in, kv_blk, g_blk, acc_q, acc_k, acc_v,
                peer_f, peer_b, th_f, th_b, in_b1, pre, tz_f, tz_b, got_f, got_b,
                ez_f, ez_b, out_d, in_d, res_f, res_b, fin_f, fin_b,
                fwd_out, bwd_out, sems):
    me = lax.axis_index("ctx")
    head = lax.axis_index("head")
    core = lax.rem(me, 2)
    chip = me // 2
    x = lax.rem(chip, plane)
    z = chip // plane
    partner = me + 1 - 2 * core
    qr = half // plane

    def dev(xp, zp):
        return ((zp * plane + xp) * 2 + core, head)

    barrier = pltpu.get_barrier_semaphore()
    pl.semaphore_signal(barrier, inc=1, device_id=(partner, head), device_id_type=MESH)
    peers = 1
    for xp in range(plane):
        @pl.when(x != xp)
        def _():
            pl.semaphore_signal(barrier, inc=1, device_id=dev(xp, z), device_id_type=MESH)

        peers = peers + (x != xp).astype(jnp.int32)
    for k in range(rounds):
        shift = 1 << k

        @pl.when(z + shift < planes)
        def _():
            pl.semaphore_signal(barrier, inc=1, device_id=dev(x, z + shift), device_id_type=MESH)

        @pl.when(z >= shift)
        def _():
            pl.semaphore_signal(barrier, inc=1, device_id=dev(x, z - shift), device_id_type=MESH)

        peers = peers + (z + shift < planes).astype(jnp.int32) + (z >= shift).astype(jnp.int32)

    loads = [pltpu.make_async_copy(hbm, ref, io_sems.at[i])
             for i, (hbm, ref) in enumerate(zip((q_hbm, k_hbm, v_hbm, d_hbm), (q_ref, k_ref, v_ref, d_ref)))]
    for copy in loads:
        copy.start()
    for copy in loads:
        copy.wait()

    blk = GROUP
    dim = HEAD_DIM

    def cut(ref, n, h):
        return ref[n * blk:(n + 1) * blk, h * dim:(h + 1) * dim]

    for h in range(heads):
        rows = slice(h * dim, (h + 1) * dim)
        for n in range(nblocks):
            kv_blk[n, rows, :] = _dot(cut(v_ref, n, h), cut(k_ref, n, h), ta=True)
            g_blk[n, rows, :] = _dot(cut(d_ref, n, h), cut(q_ref, n, h), ta=True)
        kv_sum = kv_blk[0, rows, :]
        g_sum = g_blk[0, rows, :]
        for n in range(1, nblocks):
            kv_sum = kv_sum + kv_blk[n, rows, :]
            g_sum = g_sum + g_blk[n, rows, :]
        fwd_in[rows, :] = kv_sum
        bwd_in[rows, :] = g_sum

    pl.semaphore_wait(barrier, peers)

    def remote(src, dst, sem_send, sem_recv, device):
        return pltpu.make_async_remote_copy(
            src_ref=src, dst_ref=dst, send_sem=sem_send, recv_sem=sem_recv,
            device_id=device, device_id_type=MESH)

    first = (remote(fwd_in, peer_f, sems.at[0, 0, 0, 0], sems.at[1, 0, 0, 0], (partner, head)),
             remote(bwd_in, peer_b, sems.at[0, 0, 1, 0], sems.at[1, 0, 1, 0], (partner, head)))
    for copy in first:
        copy.start()

    later = lax.broadcasted_iota(jnp.int32, (blk, blk), 0)
    earlier = lax.broadcasted_iota(jnp.int32, (blk, blk), 1)
    causal = later >= earlier
    for h in range(heads):
        for n in range(nblocks):
            qb, kb, vb, db = (cut(r, n, h) for r in (q_ref, k_ref, v_ref, d_ref))
            scores = jnp.where(causal, _dot(qb, kb, tb=True) * scale, 0.0).astype(jnp.bfloat16)
            dscores = jnp.where(causal, _dot(db, vb, tb=True), 0.0).astype(jnp.bfloat16)
            out_rows = slice(n * blk, (n + 1) * blk)
            out_cols = slice(h * dim, (h + 1) * dim)
            acc_q[out_rows, out_cols] = _dot(dscores, kb)
            acc_k[out_rows, out_cols] = _dot(dscores, qb, ta=True)
            acc_v[out_rows, out_cols] = _dot(scores, db, ta=True)

    for copy in first:
        copy.wait_recv()

    for mine in range(2):
        rows = pl.ds(mine * half, half)

        @pl.when(core == mine)
        def _():
            th_f[...] = fwd_in[rows, :] + peer_f[rows, :]
            th_b[...] = bwd_in[rows, :] + peer_b[rows, :]

    halves = (th_f, th_b)

    def scatter(s, xp):
        return remote(halves[s].at[pl.ds(xp * qr, qr)], in_b1.at[s, x],
                      sems.at[0, 2, s, xp], sems.at[1, 2, s, x], dev(xp, z))

    def scatter_in(s, xp):
        return remote(halves[s].at[pl.ds(xp * qr, qr)], in_b1.at[s, xp],
                      sems.at[0, 2, s, xp], sems.at[1, 2, s, xp], dev(xp, z))

    for s in range(2):
        for xp in range(plane):
            @pl.when(x != xp)
            def _():
                scatter(s, xp).start()
    for s in range(2):
        in_b1[s, x] = halves[s][pl.ds(x * qr, qr), :]
    for s in range(2):
        for xp in range(plane):
            @pl.when(x != xp)
            def _():
                scatter_in(s, xp).wait_recv()

    run = jnp.zeros((qr, HEAD_DIM), jnp.float32)
    for xp in range(plane):
        pre[0, xp] = run
        run = run + in_b1[0, xp]
    tz_f[0] = run
    run = jnp.zeros((qr, HEAD_DIM), jnp.float32)
    for xp in reversed(range(plane)):
        pre[1, xp] = run
        run = run + in_b1[1, xp]
    tz_b[0] = run

    ez_f[...] = jnp.zeros_like(ez_f)
    ez_b[...] = jnp.zeros_like(ez_b)

    def z_copies(k):
        shift = 1 << k
        up = remote(tz_f.at[k], got_f.at[k], sems.at[0, 3, 0, k], sems.at[1, 3, 0, k], dev(x, z + shift))
        down = remote(tz_b.at[k], got_b.at[k], sems.at[0, 3, 1, k], sems.at[1, 3, 1, k], dev(x, z - shift))
        return up, down

    for k in range(rounds):
        shift = 1 << k
        up, down = z_copies(k)
        last = k == rounds - 1

        @pl.when(z + shift < planes)
        def _():
            up.start()

        @pl.when(z >= shift)
        def _():
            down.start()

        @pl.when(z >= shift)
        def _():
            up.wait_recv()
            got = got_f[k]
            ez_f[...] += got
            if not last:
                tz_f[k + 1] = tz_f[k] + got

        @pl.when(z < shift)
        def _():
            if not last:
                tz_f[k + 1] = tz_f[k]

        @pl.when(z + shift < planes)
        def _():
            down.wait_recv()
            got = got_b[k]
            ez_b[...] += got
            if not last:
                tz_b[k + 1] = tz_b[k] + got

        @pl.when(z + shift >= planes)
        def _():
            if not last:
                tz_b[k + 1] = tz_b[k]

    zs = (ez_f, ez_b)
    for s in range(2):
        for xp in range(plane):
            out_d[s, xp] = zs[s][...] + pre[s, xp]

    def gather(s, xp):
        return remote(out_d.at[s, xp], in_d.at[s, x],
                      sems.at[0, 4, s, xp], sems.at[1, 4, s, x], dev(xp, z))

    def gather_in(s, xp):
        return remote(out_d.at[s, xp], in_d.at[s, xp],
                      sems.at[0, 4, s, xp], sems.at[1, 4, s, xp], dev(xp, z))

    for s in range(2):
        for xp in range(plane):
            @pl.when(x != xp)
            def _():
                gather(s, xp).start()
    results = (res_f, res_b)
    for s in range(2):
        results[s][pl.ds(x * qr, qr), :] = out_d[s, x]
    for s in range(2):
        for xp in range(plane):
            @pl.when(x != xp)
            def _():
                gather_in(s, xp).wait_recv()
                results[s][xp * qr:(xp + 1) * qr, :] = in_d[s, xp]

    last_pair = (remote(res_f, fin_f, sems.at[0, 1, 0, 0], sems.at[1, 1, 0, 0], (partner, head)),
                 remote(res_b, fin_b, sems.at[0, 1, 1, 0], sems.at[1, 1, 1, 0], (partner, head)))
    for copy in last_pair:
        copy.start()
    for copy in last_pair:
        copy.wait_recv()

    for mine in range(2):
        rows = pl.ds(mine * half, half)
        other = pl.ds((1 - mine) * half, half)

        @pl.when(core == mine)
        def _():
            if mine == 0:
                fwd_out[rows, :] = res_f[...]
                fwd_out[other, :] = fin_f[...]
                bwd_out[rows, :] = res_b[...] + peer_b[rows, :]
                bwd_out[other, :] = fin_b[...] + peer_b[other, :]
            else:
                fwd_out[rows, :] = res_f[...] + peer_f[rows, :]
                fwd_out[other, :] = fin_f[...] + peer_f[other, :]
                bwd_out[rows, :] = res_b[...]
                bwd_out[other, :] = fin_b[...]

    for h in range(heads):
        rows = slice(h * dim, (h + 1) * dim)
        kv_in = fwd_out[rows, :]
        kv_states = []
        for n in range(nblocks):
            kv_states.append(kv_in)
            if n + 1 < nblocks:
                kv_in = kv_in + kv_blk[n, rows, :]
        g_in = bwd_out[rows, :]
        g_states = [None] * nblocks
        for n in reversed(range(nblocks)):
            g_states[n] = g_in
            if n > 0:
                g_in = g_in + g_blk[n, rows, :]
        for n in range(nblocks):
            out_rows = slice(n * blk, (n + 1) * blk)
            out_cols = slice(h * dim, (h + 1) * dim)
            kf = cut(k_ref, n, h).astype(jnp.float32)
            vf = cut(v_ref, n, h).astype(jnp.float32)
            df = cut(d_ref, n, h).astype(jnp.float32)
            kv_s = kv_states[n]
            g_s = g_states[n]
            gq_ref[out_rows, out_cols] = (
                scale * (acc_q[out_rows, out_cols] + _dot(df, kv_s, precise=True))
            ).astype(gq_ref.dtype)
            gk_ref[out_rows, out_cols] = (
                scale * (acc_k[out_rows, out_cols] + _dot(vf, g_s, precise=True))
            ).astype(gk_ref.dtype)
            gv_ref[out_rows, out_cols] = (
                acc_v[out_rows, out_cols] + scale * _dot(kf, g_s, tb=True, precise=True)
            ).astype(gv_ref.dtype)

    stores = [pltpu.make_async_copy(ref, hbm, io_sems.at[4 + i])
              for i, (ref, hbm) in enumerate(zip((gq_ref, gk_ref, gv_ref), (gq_hbm, gk_hbm, gv_hbm)))]
    for copy in stores:
        copy.start()
    for copy in first + last_pair:
        copy.wait_send()
    for s in range(2):
        for xp in range(plane):
            @pl.when(x != xp)
            def _():
                scatter(s, xp).wait_send()
                gather(s, xp).wait_send()
    for k in range(rounds):
        shift = 1 << k
        up, down = z_copies(k)

        @pl.when(z + shift < planes)
        def _():
            up.wait_send()

        @pl.when(z >= shift)
        def _():
            down.wait_send()
    for copy in stores:
        copy.wait()


PLANE = 4
VMEM_ALL = 67043328


def core_math(q_all, k_all, v_all, d_all, scale):
    count = lax.axis_size("ctx")
    chips = count // 2
    plane = PLANE if chips % PLANE == 0 else 1
    planes = chips // plane
    rounds = max(1, (planes - 1).bit_length())
    tokens, width = q_all.shape
    heads = width // HEAD_DIM
    nblocks = tokens // GROUP
    rows = heads * HEAD_DIM
    half = rows // 2
    qr = half // plane
    cols = HEAD_DIM
    anywhere = pl.BlockSpec(memory_space=pl.ANY)
    f32 = jnp.float32
    return pl.pallas_call(
        functools.partial(core_kernel, plane, planes, rounds, half, nblocks, heads, scale),
        out_shape=(jax.ShapeDtypeStruct(q_all.shape, q_all.dtype),) * 3,
        in_specs=[anywhere] * 4,
        out_specs=(anywhere,) * 3,
        scratch_shapes=[
            *[pltpu.VMEM((tokens, width), q_all.dtype) for _ in range(7)],
            pltpu.SemaphoreType.DMA((7,)),
            pltpu.VMEM((rows, cols), f32),
            pltpu.VMEM((rows, cols), f32),
            pltpu.VMEM((nblocks, rows, cols), f32),
            pltpu.VMEM((nblocks, rows, cols), f32),
            pltpu.VMEM((tokens, width), f32),
            pltpu.VMEM((tokens, width), f32),
            pltpu.VMEM((tokens, width), f32),
            pltpu.VMEM((rows, cols), f32),
            pltpu.VMEM((rows, cols), f32),
            pltpu.VMEM((half, cols), f32),
            pltpu.VMEM((half, cols), f32),
            pltpu.VMEM((2, plane, qr, cols), f32),
            pltpu.VMEM((2, plane, qr, cols), f32),
            pltpu.VMEM((rounds, qr, cols), f32),
            pltpu.VMEM((rounds, qr, cols), f32),
            pltpu.VMEM((rounds, qr, cols), f32),
            pltpu.VMEM((rounds, qr, cols), f32),
            pltpu.VMEM((qr, cols), f32),
            pltpu.VMEM((qr, cols), f32),
            pltpu.VMEM((2, plane, qr, cols), f32),
            pltpu.VMEM((2, plane, qr, cols), f32),
            pltpu.VMEM((half, cols), f32),
            pltpu.VMEM((half, cols), f32),
            pltpu.VMEM((half, cols), f32),
            pltpu.VMEM((half, cols), f32),
            pltpu.VMEM((rows, cols), f32),
            pltpu.VMEM((rows, cols), f32),
            pltpu.SemaphoreType.DMA((2, 5, 2, max(plane, rounds))),
        ],
        compiler_params=pltpu.CompilerParams(collective_id=0, has_side_effects=True,
                                             vmem_limit_bytes=VMEM_ALL),
    )(q_all, k_all, v_all, d_all)


def exchange_kernel(count, n_arrays, src_cut, dst_cut, *refs):
    srcs = refs[:n_arrays]
    dsts = refs[n_arrays:2 * n_arrays]
    send_sems, recv_sems, local_sems = refs[2 * n_arrays:]
    me = lax.axis_index("head")
    place = lax.axis_index("ctx")
    barrier = pltpu.get_barrier_semaphore()
    for j in range(count):
        @pl.when(me != j)
        def _():
            pl.semaphore_signal(barrier, inc=1, device_id=(place, j), device_id_type=MESH)
    pl.semaphore_wait(barrier, count - 1)

    def remote(a, j, dst_index):
        return pltpu.make_async_remote_copy(
            src_ref=src_cut(srcs[a], j), dst_ref=dst_cut(dsts[a], dst_index),
            send_sem=send_sems.at[a, j], recv_sem=recv_sems.at[a, me],
            device_id=(place, j), device_id_type=MESH)

    for a in range(n_arrays):
        local = pltpu.make_async_copy(src_cut(srcs[a], me), dst_cut(dsts[a], me), local_sems.at[a])
        local.start()
    for step in range(1, count):
        for a in range(n_arrays):
            j_dyn = lax.rem(me + step, count)
            for j in range(count):
                @pl.when(j_dyn == j)
                def _():
                    remote(a, j, me).start()
    for a in range(n_arrays):
        pltpu.make_async_copy(src_cut(srcs[a], me), dst_cut(dsts[a], me), local_sems.at[a]).wait()
    for a in range(n_arrays):
        for j in range(count):
            @pl.when(me != j)
            def _():
                copy = pltpu.make_async_remote_copy(
                    src_ref=src_cut(srcs[a], j), dst_ref=dst_cut(dsts[a], j),
                    send_sem=send_sems.at[a, j], recv_sem=recv_sems.at[a, j],
                    device_id=(place, j), device_id_type=MESH)
                copy.wait_send()
                copy.wait_recv()


def exchange(arrays, out_shape, src_cut, dst_cut, collective_id, in_space, out_space):
    count = lax.axis_size("head")
    if count == 1:
        return tuple(arrays)
    n_arrays = len(arrays)
    in_spec = pl.BlockSpec(memory_space=in_space)
    out_spec = pl.BlockSpec(memory_space=out_space)
    return pl.pallas_call(
        functools.partial(exchange_kernel, count, n_arrays, src_cut, dst_cut),
        out_shape=tuple(jax.ShapeDtypeStruct(out_shape, arrays[0].dtype) for _ in arrays),
        in_specs=[in_spec] * n_arrays,
        out_specs=tuple(out_spec for _ in arrays),
        scratch_shapes=[
            pltpu.SemaphoreType.DMA((n_arrays, count)),
            pltpu.SemaphoreType.DMA((n_arrays, count)),
            pltpu.SemaphoreType.DMA((n_arrays,)),
        ],
        compiler_params=pltpu.CompilerParams(collective_id=collective_id, has_side_effects=True,
                                             vmem_limit_bytes=VMEM_ALL),
    )(*arrays)


def per_device(queries, key_rows, value_rows, grad_out):
    count = lax.axis_size("head")
    rows_in, width = queries.shape
    cols = width // count
    q_all, k_all, v_all, d_all = exchange(
        (queries, key_rows, value_rows, grad_out),
        (rows_in * count, cols),
        lambda ref, j: ref.at[:, pl.ds(j * cols, cols)],
        lambda ref, j: ref.at[pl.ds(j * rows_in, rows_in), :],
        1,
        pl.ANY,
        pl.ANY,
    )
    rows_here = q_all.shape[0]
    scale = (HEAD_DIM * rows_here * lax.axis_size("ctx")) ** (-0.5)
    grad_q, grad_k, grad_v = core_math(q_all, k_all, v_all, d_all, scale)
    result_q, result_k, result_v = exchange(
        (grad_q, grad_k, grad_v),
        (rows_in, width),
        lambda ref, j: ref.at[pl.ds(j * rows_in, rows_in), :],
        lambda ref, j: ref.at[:, pl.ds(j * cols, cols)],
        2,
        pl.ANY,
        pl.ANY,
    )
    return (result_q, result_k, result_v)


def solution(mesh):
    placed = (
        P(("ctx", "head"), None),
        P(("ctx", "head"), None),
        P(("ctx", "head"), None),
        P(("ctx", "head"), None),
    )
    return jax.shard_map(
        per_device,
        mesh=mesh,
        in_specs=placed,
        out_specs=(P(("ctx", "head"), None), P(("ctx", "head"), None), P(("ctx", "head"), None)),
        check_vma=False,
    )
```

```python
import functools

import jax
import jax.numpy as jnp
from jax import lax
from jax.experimental import pallas as pl
from jax.experimental.pallas import tpu as pltpu
from jax.sharding import PartitionSpec as P

HEAD_DIM = 128
GROUP = 128


MESH = pl.DeviceIdType.MESH


def _dot(a, b, ta=False, tb=False, precise=False):
    dims = (((0 if ta else 1,), (1 if tb else 0,)), ((), ()))
    return lax.dot_general(a, b, dims, preferred_element_type=jnp.float32,
                           precision=lax.Precision.HIGHEST if precise else None)


def core_kernel(plane, planes, rounds, half, nblocks, heads, scale,
                q_hbm, k_hbm, v_hbm, d_hbm, gq_hbm, gk_hbm, gv_hbm,
                q_ref, k_ref, v_ref, d_ref, gq_ref, gk_ref, gv_ref, io_sems,
                fwd_in, bwd_in, kv_blk, g_blk, acc_q, acc_k, acc_v,
                peer_f, peer_b, th_f, th_b, in_b1, pre, tz_f, tz_b, got_f, got_b,
                ez_f, ez_b, out_d, in_d, res_f, res_b, fin_f, fin_b,
                fwd_out, bwd_out, sems):
    me = lax.axis_index("ctx")
    head = lax.axis_index("head")
    core = lax.rem(me, 2)
    chip = me // 2
    x = lax.rem(chip, plane)
    z = chip // plane
    partner = me + 1 - 2 * core
    qr = half // plane

    def dev(xp, zp):
        return ((zp * plane + xp) * 2 + core, head)

    barrier = pltpu.get_barrier_semaphore()
    pl.semaphore_signal(barrier, inc=1, device_id=(partner, head), device_id_type=MESH)
    peers = 1
    for xp in range(plane):
        @pl.when(x != xp)
        def _():
            pl.semaphore_signal(barrier, inc=1, device_id=dev(xp, z), device_id_type=MESH)

        peers = peers + (x != xp).astype(jnp.int32)
    for k in range(rounds):
        shift = 1 << k

        @pl.when(z + shift < planes)
        def _():
            pl.semaphore_signal(barrier, inc=1, device_id=dev(x, z + shift), device_id_type=MESH)

        @pl.when(z >= shift)
        def _():
            pl.semaphore_signal(barrier, inc=1, device_id=dev(x, z - shift), device_id_type=MESH)

        peers = peers + (z + shift < planes).astype(jnp.int32) + (z >= shift).astype(jnp.int32)

    loads = [pltpu.make_async_copy(hbm, ref, io_sems.at[i])
             for i, (hbm, ref) in enumerate(zip((q_hbm, k_hbm, v_hbm, d_hbm), (q_ref, k_ref, v_ref, d_ref)))]
    for copy in loads:
        copy.start()
    for copy in loads:
        copy.wait()

    blk = GROUP
    dim = HEAD_DIM

    def cut(ref, n, h):
        return ref[n * blk:(n + 1) * blk, h * dim:(h + 1) * dim]

    for h in range(heads):
        rows = slice(h * dim, (h + 1) * dim)
        for n in range(nblocks):
            kv_blk[n, rows, :] = _dot(cut(v_ref, n, h), cut(k_ref, n, h), ta=True)
            g_blk[n, rows, :] = _dot(cut(d_ref, n, h), cut(q_ref, n, h), ta=True)
        kv_sum = kv_blk[0, rows, :]
        g_sum = g_blk[0, rows, :]
        for n in range(1, nblocks):
            kv_sum = kv_sum + kv_blk[n, rows, :]
            g_sum = g_sum + g_blk[n, rows, :]
        fwd_in[rows, :] = kv_sum
        bwd_in[rows, :] = g_sum

    pl.semaphore_wait(barrier, peers)

    def remote(src, dst, sem_send, sem_recv, device):
        return pltpu.make_async_remote_copy(
            src_ref=src, dst_ref=dst, send_sem=sem_send, recv_sem=sem_recv,
            device_id=device, device_id_type=MESH)

    first = (remote(fwd_in, peer_f, sems.at[0, 0, 0, 0], sems.at[1, 0, 0, 0], (partner, head)),
             remote(bwd_in, peer_b, sems.at[0, 0, 1, 0], sems.at[1, 0, 1, 0], (partner, head)))
    for copy in first:
        copy.start()

    later = lax.broadcasted_iota(jnp.int32, (blk, blk), 0)
    earlier = lax.broadcasted_iota(jnp.int32, (blk, blk), 1)
    causal = later >= earlier
    for h in range(heads):
        for n in range(nblocks):
            qb, kb, vb, db = (cut(r, n, h) for r in (q_ref, k_ref, v_ref, d_ref))
            scores = jnp.where(causal, _dot(qb, kb, tb=True) * scale, 0.0).astype(jnp.bfloat16)
            dscores = jnp.where(causal, _dot(db, vb, tb=True), 0.0).astype(jnp.bfloat16)
            out_rows = slice(n * blk, (n + 1) * blk)
            out_cols = slice(h * dim, (h + 1) * dim)
            acc_q[out_rows, out_cols] = _dot(dscores, kb)
            acc_k[out_rows, out_cols] = _dot(dscores, qb, ta=True)
            acc_v[out_rows, out_cols] = _dot(scores, db, ta=True)

    for copy in first:
        copy.wait_recv()

    for mine in range(2):
        rows = pl.ds(mine * half, half)

        @pl.when(core == mine)
        def _():
            th_f[...] = fwd_in[rows, :] + peer_f[rows, :]
            th_b[...] = bwd_in[rows, :] + peer_b[rows, :]

    halves = (th_f, th_b)

    def scatter(s, xp):
        return remote(halves[s].at[pl.ds(xp * qr, qr)], in_b1.at[s, x],
                      sems.at[0, 2, s, xp], sems.at[1, 2, s, x], dev(xp, z))

    def scatter_in(s, xp):
        return remote(halves[s].at[pl.ds(xp * qr, qr)], in_b1.at[s, xp],
                      sems.at[0, 2, s, xp], sems.at[1, 2, s, xp], dev(xp, z))

    for s in range(2):
        for xp in range(plane):
            @pl.when(x != xp)
            def _():
                scatter(s, xp).start()
    for s in range(2):
        in_b1[s, x] = halves[s][pl.ds(x * qr, qr), :]
    for s in range(2):
        for xp in range(plane):
            @pl.when(x != xp)
            def _():
                scatter_in(s, xp).wait_recv()

    run = jnp.zeros((qr, HEAD_DIM), jnp.float32)
    for xp in range(plane):
        pre[0, xp] = run
        run = run + in_b1[0, xp]
    tz_f[0] = run
    run = jnp.zeros((qr, HEAD_DIM), jnp.float32)
    for xp in reversed(range(plane)):
        pre[1, xp] = run
        run = run + in_b1[1, xp]
    tz_b[0] = run

    ez_f[...] = jnp.zeros_like(ez_f)
    ez_b[...] = jnp.zeros_like(ez_b)

    def z_copies(k):
        shift = 1 << k
        up = remote(tz_f.at[k], got_f.at[k], sems.at[0, 3, 0, k], sems.at[1, 3, 0, k], dev(x, z + shift))
        down = remote(tz_b.at[k], got_b.at[k], sems.at[0, 3, 1, k], sems.at[1, 3, 1, k], dev(x, z - shift))
        return up, down

    for k in range(rounds):
        shift = 1 << k
        up, down = z_copies(k)
        last = k == rounds - 1

        @pl.when(z + shift < planes)
        def _():
            up.start()

        @pl.when(z >= shift)
        def _():
            down.start()

        @pl.when(z >= shift)
        def _():
            up.wait_recv()
            got = got_f[k]
            ez_f[...] += got
            if not last:
                tz_f[k + 1] = tz_f[k] + got

        @pl.when(z < shift)
        def _():
            if not last:
                tz_f[k + 1] = tz_f[k]

        @pl.when(z + shift < planes)
        def _():
            down.wait_recv()
            got = got_b[k]
            ez_b[...] += got
            if not last:
                tz_b[k + 1] = tz_b[k] + got

        @pl.when(z + shift >= planes)
        def _():
            if not last:
                tz_b[k + 1] = tz_b[k]

    zs = (ez_f, ez_b)
    for s in range(2):
        for xp in range(plane):
            out_d[s, xp] = zs[s][...] + pre[s, xp]

    def gather(s, xp):
        return remote(out_d.at[s, xp], in_d.at[s, x],
                      sems.at[0, 4, s, xp], sems.at[1, 4, s, x], dev(xp, z))

    def gather_in(s, xp):
        return remote(out_d.at[s, xp], in_d.at[s, xp],
                      sems.at[0, 4, s, xp], sems.at[1, 4, s, xp], dev(xp, z))

    for s in range(2):
        for xp in range(plane):
            @pl.when(x != xp)
            def _():
                gather(s, xp).start()
    results = (res_f, res_b)
    for s in range(2):
        results[s][pl.ds(x * qr, qr), :] = out_d[s, x]
    for s in range(2):
        for xp in range(plane):
            @pl.when(x != xp)
            def _():
                gather_in(s, xp).wait_recv()
                results[s][xp * qr:(xp + 1) * qr, :] = in_d[s, xp]

    last_pair = (remote(res_f, fin_f, sems.at[0, 1, 0, 0], sems.at[1, 1, 0, 0], (partner, head)),
                 remote(res_b, fin_b, sems.at[0, 1, 1, 0], sems.at[1, 1, 1, 0], (partner, head)))
    for copy in last_pair:
        copy.start()
    for copy in last_pair:
        copy.wait_recv()

    for mine in range(2):
        rows = pl.ds(mine * half, half)
        other = pl.ds((1 - mine) * half, half)

        @pl.when(core == mine)
        def _():
            if mine == 0:
                fwd_out[rows, :] = res_f[...]
                fwd_out[other, :] = fin_f[...]
                bwd_out[rows, :] = res_b[...] + peer_b[rows, :]
                bwd_out[other, :] = fin_b[...] + peer_b[other, :]
            else:
                fwd_out[rows, :] = res_f[...] + peer_f[rows, :]
                fwd_out[other, :] = fin_f[...] + peer_f[other, :]
                bwd_out[rows, :] = res_b[...]
                bwd_out[other, :] = fin_b[...]

    for h in range(heads):
        rows = slice(h * dim, (h + 1) * dim)
        kv_in = fwd_out[rows, :]
        kv_states = []
        for n in range(nblocks):
            kv_states.append(kv_in)
            if n + 1 < nblocks:
                kv_in = kv_in + kv_blk[n, rows, :]
        g_in = bwd_out[rows, :]
        g_states = [None] * nblocks
        for n in reversed(range(nblocks)):
            g_states[n] = g_in
            if n > 0:
                g_in = g_in + g_blk[n, rows, :]
        for n in range(nblocks):
            out_rows = slice(n * blk, (n + 1) * blk)
            out_cols = slice(h * dim, (h + 1) * dim)
            kf = cut(k_ref, n, h).astype(jnp.float32)
            vf = cut(v_ref, n, h).astype(jnp.float32)
            df = cut(d_ref, n, h).astype(jnp.float32)
            kv_s = kv_states[n]
            g_s = g_states[n]
            gq_ref[out_rows, out_cols] = (
                scale * (acc_q[out_rows, out_cols] + _dot(df, kv_s, precise=True))
            ).astype(gq_ref.dtype)
            gk_ref[out_rows, out_cols] = (
                scale * (acc_k[out_rows, out_cols] + _dot(vf, g_s, precise=True))
            ).astype(gk_ref.dtype)
            gv_ref[out_rows, out_cols] = (
                acc_v[out_rows, out_cols] + scale * _dot(kf, g_s, tb=True, precise=True)
            ).astype(gv_ref.dtype)

    stores = [pltpu.make_async_copy(ref, hbm, io_sems.at[4 + i])
              for i, (ref, hbm) in enumerate(zip((gq_ref, gk_ref, gv_ref), (gq_hbm, gk_hbm, gv_hbm)))]
    for copy in stores:
        copy.start()
    for copy in first + last_pair:
        copy.wait_send()
    for s in range(2):
        for xp in range(plane):
            @pl.when(x != xp)
            def _():
                scatter(s, xp).wait_send()
                gather(s, xp).wait_send()
    for k in range(rounds):
        shift = 1 << k
        up, down = z_copies(k)

        @pl.when(z + shift < planes)
        def _():
            up.wait_send()

        @pl.when(z >= shift)
        def _():
            down.wait_send()
    for copy in stores:
        copy.wait()


PLANE = 4
VMEM_ALL = 67043328


def core_math(q_all, k_all, v_all, d_all, scale):
    count = lax.axis_size("ctx")
    chips = count // 2
    plane = PLANE if chips % PLANE == 0 else 1
    planes = chips // plane
    rounds = max(1, (planes - 1).bit_length())
    tokens, width = q_all.shape
    heads = width // HEAD_DIM
    nblocks = tokens // GROUP
    rows = heads * HEAD_DIM
    half = rows // 2
    qr = half // plane
    cols = HEAD_DIM
    anywhere = pl.BlockSpec(memory_space=pl.ANY)
    f32 = jnp.float32
    return pl.pallas_call(
        functools.partial(core_kernel, plane, planes, rounds, half, nblocks, heads, scale),
        out_shape=(jax.ShapeDtypeStruct(q_all.shape, q_all.dtype),) * 3,
        in_specs=[anywhere] * 4,
        out_specs=(anywhere,) * 3,
        scratch_shapes=[
            *[pltpu.VMEM((tokens, width), q_all.dtype) for _ in range(7)],
            pltpu.SemaphoreType.DMA((7,)),
            pltpu.VMEM((rows, cols), f32),
            pltpu.VMEM((rows, cols), f32),
            pltpu.VMEM((nblocks, rows, cols), f32),
            pltpu.VMEM((nblocks, rows, cols), f32),
            pltpu.VMEM((tokens, width), f32),
            pltpu.VMEM((tokens, width), f32),
            pltpu.VMEM((tokens, width), f32),
            pltpu.VMEM((rows, cols), f32),
            pltpu.VMEM((rows, cols), f32),
            pltpu.VMEM((half, cols), f32),
            pltpu.VMEM((half, cols), f32),
            pltpu.VMEM((2, plane, qr, cols), f32),
            pltpu.VMEM((2, plane, qr, cols), f32),
            pltpu.VMEM((rounds, qr, cols), f32),
            pltpu.VMEM((rounds, qr, cols), f32),
            pltpu.VMEM((rounds, qr, cols), f32),
            pltpu.VMEM((rounds, qr, cols), f32),
            pltpu.VMEM((qr, cols), f32),
            pltpu.VMEM((qr, cols), f32),
            pltpu.VMEM((2, plane, qr, cols), f32),
            pltpu.VMEM((2, plane, qr, cols), f32),
            pltpu.VMEM((half, cols), f32),
            pltpu.VMEM((half, cols), f32),
            pltpu.VMEM((half, cols), f32),
            pltpu.VMEM((half, cols), f32),
            pltpu.VMEM((rows, cols), f32),
            pltpu.VMEM((rows, cols), f32),
            pltpu.SemaphoreType.DMA((2, 5, 2, max(plane, rounds))),
        ],
        compiler_params=pltpu.CompilerParams(collective_id=0, has_side_effects=True,
                                             vmem_limit_bytes=VMEM_ALL),
    )(q_all, k_all, v_all, d_all)


def exchange_kernel(count, n_arrays, rows, src_cut, dst_cut, *refs):
    srcs = refs[:n_arrays]
    dsts = refs[n_arrays:2 * n_arrays]
    send_sems, recv_sems, local_sems, relay_buf, relay_sems = refs[2 * n_arrays:]
    me = lax.axis_index("head")
    place = lax.axis_index("ctx")
    far = count // 2 if count % 2 == 0 and count >= 4 else None
    hr = rows // 2
    barrier = pltpu.get_barrier_semaphore()
    for j in range(count):
        @pl.when(me != j)
        def _():
            pl.semaphore_signal(barrier, inc=1, device_id=(place, j), device_id_type=MESH)
    pl.semaphore_wait(barrier, count - 1)

    def peer(step):
        return lax.rem(me + step, count)

    def copy(src, dst, sem_send, sem_recv, j):
        return pltpu.make_async_remote_copy(
            src_ref=src, dst_ref=dst, send_sem=sem_send, recv_sem=sem_recv,
            device_id=(place, j), device_id_type=MESH)

    def direct(a, step):
        return copy(src_cut(srcs[a], peer(step), 0, rows), dst_cut(dsts[a], me, 0, rows),
                    send_sems.at[a, step], recv_sems.at[a, step], peer(step))

    def direct_in(a, step):
        return copy(src_cut(srcs[a], peer(step), 0, rows),
                    dst_cut(dsts[a], peer(count - step), 0, rows),
                    send_sems.at[a, step], recv_sems.at[a, step], peer(step))

    steps = [s for s in range(1, count) if s != far]
    for step in steps:
        for a in range(n_arrays):
            direct(a, step).start()

    def leg_one(a, side):
        first_row = 0 if side == 0 else hr
        relay = peer(1) if side == 0 else peer(count - 1)
        return copy(src_cut(srcs[a], peer(far), first_row, hr), relay_buf.at[side, a],
                    relay_sems.at[0, 0, side, a], relay_sems.at[1, 0, side, a], relay)

    def leg_two(a, side):
        if side == 0:
            origin, first_row, target = peer(count - 1), 0, peer(far - 1)
        else:
            origin, first_row, target = peer(1), hr, peer(count - far + 1)
        return copy(relay_buf.at[side, a], dst_cut(dsts[a], origin, first_row, hr),
                    relay_sems.at[0, 1, side, a], relay_sems.at[1, 1, side, a], target)

    def leg_two_in(a, side):
        first_row = 0 if side == 0 else hr
        return copy(relay_buf.at[side, a], dst_cut(dsts[a], peer(far), first_row, hr),
                    relay_sems.at[0, 1, side, a], relay_sems.at[1, 1, side, a], peer(far))

    if far is not None:
        for a in range(n_arrays):
            for side in range(2):
                leg_one(a, side).start()

    for a in range(n_arrays):
        pltpu.make_async_copy(src_cut(srcs[a], me, 0, rows), dst_cut(dsts[a], me, 0, rows),
                              local_sems.at[a]).start()

    if far is not None:
        for a in range(n_arrays):
            for side in range(2):
                leg_one(a, side).wait_recv()
                leg_two(a, side).start()

    for a in range(n_arrays):
        pltpu.make_async_copy(src_cut(srcs[a], me, 0, rows), dst_cut(dsts[a], me, 0, rows),
                              local_sems.at[a]).wait()
    for step in steps:
        for a in range(n_arrays):
            direct_in(a, step).wait_send()
            direct_in(a, step).wait_recv()
    if far is not None:
        for a in range(n_arrays):
            for side in range(2):
                leg_one(a, side).wait_send()
                leg_two(a, side).wait_send()
                leg_two_in(a, side).wait_recv()


def exchange(arrays, out_shape, rows, cols, src_cut, dst_cut, collective_id):
    count = lax.axis_size("head")
    if count == 1:
        return tuple(arrays)
    n_arrays = len(arrays)
    anywhere = pl.BlockSpec(memory_space=pl.ANY)
    return pl.pallas_call(
        functools.partial(exchange_kernel, count, n_arrays, rows, src_cut, dst_cut),
        out_shape=tuple(jax.ShapeDtypeStruct(out_shape, arrays[0].dtype) for _ in arrays),
        in_specs=[anywhere] * n_arrays,
        out_specs=tuple(anywhere for _ in arrays),
        scratch_shapes=[
            pltpu.SemaphoreType.DMA((n_arrays, count)),
            pltpu.SemaphoreType.DMA((n_arrays, count)),
            pltpu.SemaphoreType.DMA((n_arrays,)),
            pltpu.VMEM((2, n_arrays, rows // 2, cols), arrays[0].dtype),
            pltpu.SemaphoreType.DMA((2, 2, 2, n_arrays)),
        ],
        compiler_params=pltpu.CompilerParams(collective_id=collective_id, has_side_effects=True,
                                             vmem_limit_bytes=VMEM_ALL),
    )(*arrays)


def per_device(queries, key_rows, value_rows, grad_out):
    count = lax.axis_size("head")
    rows_in, width = queries.shape
    cols = width // count
    q_all, k_all, v_all, d_all = exchange(
        (queries, key_rows, value_rows, grad_out),
        (rows_in * count, cols),
        rows_in,
        cols,
        lambda ref, j, r0, nr: ref.at[pl.ds(r0, nr), pl.ds(j * cols, cols)],
        lambda ref, j, r0, nr: ref.at[pl.ds(j * rows_in + r0, nr), :],
        1,
    )
    rows_here = q_all.shape[0]
    scale = (HEAD_DIM * rows_here * lax.axis_size("ctx")) ** (-0.5)
    grad_q, grad_k, grad_v = core_math(q_all, k_all, v_all, d_all, scale)
    result_q, result_k, result_v = exchange(
        (grad_q, grad_k, grad_v),
        (rows_in, width),
        rows_in,
        cols,
        lambda ref, j, r0, nr: ref.at[pl.ds(j * rows_in + r0, nr), :],
        lambda ref, j, r0, nr: ref.at[pl.ds(r0, nr), pl.ds(j * cols, cols)],
        2,
    )
    return (result_q, result_k, result_v)


def solution(mesh):
    placed = (
        P(("ctx", "head"), None),
        P(("ctx", "head"), None),
        P(("ctx", "head"), None),
        P(("ctx", "head"), None),
    )
    return jax.shard_map(
        per_device,
        mesh=mesh,
        in_specs=placed,
        out_specs=(P(("ctx", "head"), None), P(("ctx", "head"), None), P(("ctx", "head"), None)),
        check_vma=False,
    )
```

```python
import functools

import jax
import jax.numpy as jnp
from jax import lax
from jax.experimental import pallas as pl
from jax.experimental.pallas import tpu as pltpu
from jax.sharding import PartitionSpec as P

HEAD_DIM = 128
GROUP = 128


MESH = pl.DeviceIdType.MESH


def _dot(a, b, ta=False, tb=False, precise=False):
    dims = (((0 if ta else 1,), (1 if tb else 0,)), ((), ()))
    return lax.dot_general(a, b, dims, preferred_element_type=jnp.float32,
                           precision=lax.Precision.HIGHEST if precise else None)


def core_kernel(plane, planes, rounds, half, nblocks, heads, scale, ways,
                q_hbm, k_hbm, v_hbm, d_hbm, gq_hbm, gk_hbm, gv_hbm,
                q_ref, k_ref, v_ref, d_ref, gq_ref, gk_ref, gv_ref, io_sems,
                fwd_in, bwd_in, kv_blk, g_blk, acc_q, acc_k, acc_v,
                peer_f, peer_b, th_f, th_b, in_b1, pre, tz_f, tz_b, got_f, got_b,
                ez_f, ez_b, out_d, in_d, res_f, res_b, fin_f, fin_b,
                fwd_out, bwd_out, sems, x_sems):
    me = lax.axis_index("ctx")
    head = lax.axis_index("head")
    core = lax.rem(me, 2)
    chip = me // 2
    x = lax.rem(chip, plane)
    z = chip // plane
    partner = me + 1 - 2 * core
    qr = half // plane

    def dev(xp, zp):
        return ((zp * plane + xp) * 2 + core, head)

    barrier = pltpu.get_barrier_semaphore()
    pl.semaphore_signal(barrier, inc=1, device_id=(partner, head), device_id_type=MESH)
    peers = 1
    for xp in range(plane):
        @pl.when(x != xp)
        def _():
            pl.semaphore_signal(barrier, inc=1, device_id=dev(xp, z), device_id_type=MESH)

        peers = peers + (x != xp).astype(jnp.int32)
    for k in range(rounds):
        shift = 1 << k

        @pl.when(z + shift < planes)
        def _():
            pl.semaphore_signal(barrier, inc=1, device_id=dev(x, z + shift), device_id_type=MESH)

        @pl.when(z >= shift)
        def _():
            pl.semaphore_signal(barrier, inc=1, device_id=dev(x, z - shift), device_id_type=MESH)

        peers = peers + (z + shift < planes).astype(jnp.int32) + (z >= shift).astype(jnp.int32)
    for j in range(ways):
        @pl.when(head != j)
        def _():
            pl.semaphore_signal(barrier, inc=1, device_id=(me, j), device_id_type=MESH)
    pl.semaphore_wait(barrier, peers + (ways - 1))

    rows_in = q_hbm.shape[0]
    cols_in = q_ref.shape[1]
    hbm_in = (q_hbm, k_hbm, v_hbm, d_hbm)
    vm_in = (q_ref, k_ref, v_ref, d_ref)

    def spread(a, j):
        return pltpu.make_async_remote_copy(
            src_ref=hbm_in[a].at[:, pl.ds(j * cols_in, cols_in)],
            dst_ref=vm_in[a].at[pl.ds(head * rows_in, rows_in)],
            send_sem=x_sems.at[0, a, j], recv_sem=x_sems.at[1, a, head],
            device_id=(me, j), device_id_type=MESH)

    def spread_in(a, j):
        return pltpu.make_async_remote_copy(
            src_ref=hbm_in[a].at[:, pl.ds(j * cols_in, cols_in)],
            dst_ref=vm_in[a].at[pl.ds(j * rows_in, rows_in)],
            send_sem=x_sems.at[0, a, j], recv_sem=x_sems.at[1, a, j],
            device_id=(me, j), device_id_type=MESH)

    loads = [pltpu.make_async_copy(hbm_in[a].at[:, pl.ds(head * cols_in, cols_in)],
                                   vm_in[a].at[pl.ds(head * rows_in, rows_in)], io_sems.at[a])
             for a in range(4)]
    for step in range(1, ways):
        for a in range(4):
            j_dyn = lax.rem(head + step, ways)
            for j in range(ways):
                @pl.when(j_dyn == j)
                def _():
                    spread(a, j).start()
    for copy in loads:
        copy.start()
    for copy in loads:
        copy.wait()
    for a in range(4):
        for j in range(ways):
            @pl.when(head != j)
            def _():
                spread_in(a, j).wait_recv()

    blk = GROUP
    dim = HEAD_DIM

    def cut(ref, n, h):
        return ref[n * blk:(n + 1) * blk, h * dim:(h + 1) * dim]

    for h in range(heads):
        rows = slice(h * dim, (h + 1) * dim)
        for n in range(nblocks):
            kv_blk[n, rows, :] = _dot(cut(v_ref, n, h), cut(k_ref, n, h), ta=True)
            g_blk[n, rows, :] = _dot(cut(d_ref, n, h), cut(q_ref, n, h), ta=True)
        kv_sum = kv_blk[0, rows, :]
        g_sum = g_blk[0, rows, :]
        for n in range(1, nblocks):
            kv_sum = kv_sum + kv_blk[n, rows, :]
            g_sum = g_sum + g_blk[n, rows, :]
        fwd_in[rows, :] = kv_sum
        bwd_in[rows, :] = g_sum


    def remote(src, dst, sem_send, sem_recv, device):
        return pltpu.make_async_remote_copy(
            src_ref=src, dst_ref=dst, send_sem=sem_send, recv_sem=sem_recv,
            device_id=device, device_id_type=MESH)

    first = (remote(fwd_in, peer_f, sems.at[0, 0, 0, 0], sems.at[1, 0, 0, 0], (partner, head)),
             remote(bwd_in, peer_b, sems.at[0, 0, 1, 0], sems.at[1, 0, 1, 0], (partner, head)))
    for copy in first:
        copy.start()

    later = lax.broadcasted_iota(jnp.int32, (blk, blk), 0)
    earlier = lax.broadcasted_iota(jnp.int32, (blk, blk), 1)
    causal = later >= earlier
    for h in range(heads):
        for n in range(nblocks):
            qb, kb, vb, db = (cut(r, n, h) for r in (q_ref, k_ref, v_ref, d_ref))
            scores = jnp.where(causal, _dot(qb, kb, tb=True) * scale, 0.0).astype(jnp.bfloat16)
            dscores = jnp.where(causal, _dot(db, vb, tb=True), 0.0).astype(jnp.bfloat16)
            out_rows = slice(n * blk, (n + 1) * blk)
            out_cols = slice(h * dim, (h + 1) * dim)
            acc_q[out_rows, out_cols] = _dot(dscores, kb)
            acc_k[out_rows, out_cols] = _dot(dscores, qb, ta=True)
            acc_v[out_rows, out_cols] = _dot(scores, db, ta=True)

    for copy in first:
        copy.wait_recv()

    for mine in range(2):
        rows = pl.ds(mine * half, half)

        @pl.when(core == mine)
        def _():
            th_f[...] = fwd_in[rows, :] + peer_f[rows, :]
            th_b[...] = bwd_in[rows, :] + peer_b[rows, :]

    halves = (th_f, th_b)

    def scatter(s, xp):
        return remote(halves[s].at[pl.ds(xp * qr, qr)], in_b1.at[s, x],
                      sems.at[0, 2, s, xp], sems.at[1, 2, s, x], dev(xp, z))

    def scatter_in(s, xp):
        return remote(halves[s].at[pl.ds(xp * qr, qr)], in_b1.at[s, xp],
                      sems.at[0, 2, s, xp], sems.at[1, 2, s, xp], dev(xp, z))

    for s in range(2):
        for xp in range(plane):
            @pl.when(x != xp)
            def _():
                scatter(s, xp).start()
    for s in range(2):
        in_b1[s, x] = halves[s][pl.ds(x * qr, qr), :]
    for s in range(2):
        for xp in range(plane):
            @pl.when(x != xp)
            def _():
                scatter_in(s, xp).wait_recv()

    run = jnp.zeros((qr, HEAD_DIM), jnp.float32)
    for xp in range(plane):
        pre[0, xp] = run
        run = run + in_b1[0, xp]
    tz_f[0] = run
    run = jnp.zeros((qr, HEAD_DIM), jnp.float32)
    for xp in reversed(range(plane)):
        pre[1, xp] = run
        run = run + in_b1[1, xp]
    tz_b[0] = run

    ez_f[...] = jnp.zeros_like(ez_f)
    ez_b[...] = jnp.zeros_like(ez_b)

    def z_copies(k):
        shift = 1 << k
        up = remote(tz_f.at[k], got_f.at[k], sems.at[0, 3, 0, k], sems.at[1, 3, 0, k], dev(x, z + shift))
        down = remote(tz_b.at[k], got_b.at[k], sems.at[0, 3, 1, k], sems.at[1, 3, 1, k], dev(x, z - shift))
        return up, down

    for k in range(rounds):
        shift = 1 << k
        up, down = z_copies(k)
        last = k == rounds - 1

        @pl.when(z + shift < planes)
        def _():
            up.start()

        @pl.when(z >= shift)
        def _():
            down.start()

        @pl.when(z >= shift)
        def _():
            up.wait_recv()
            got = got_f[k]
            ez_f[...] += got
            if not last:
                tz_f[k + 1] = tz_f[k] + got

        @pl.when(z < shift)
        def _():
            if not last:
                tz_f[k + 1] = tz_f[k]

        @pl.when(z + shift < planes)
        def _():
            down.wait_recv()
            got = got_b[k]
            ez_b[...] += got
            if not last:
                tz_b[k + 1] = tz_b[k] + got

        @pl.when(z + shift >= planes)
        def _():
            if not last:
                tz_b[k + 1] = tz_b[k]

    zs = (ez_f, ez_b)
    for s in range(2):
        for xp in range(plane):
            out_d[s, xp] = zs[s][...] + pre[s, xp]

    def gather(s, xp):
        return remote(out_d.at[s, xp], in_d.at[s, x],
                      sems.at[0, 4, s, xp], sems.at[1, 4, s, x], dev(xp, z))

    def gather_in(s, xp):
        return remote(out_d.at[s, xp], in_d.at[s, xp],
                      sems.at[0, 4, s, xp], sems.at[1, 4, s, xp], dev(xp, z))

    for s in range(2):
        for xp in range(plane):
            @pl.when(x != xp)
            def _():
                gather(s, xp).start()
    results = (res_f, res_b)
    for s in range(2):
        results[s][pl.ds(x * qr, qr), :] = out_d[s, x]
    for s in range(2):
        for xp in range(plane):
            @pl.when(x != xp)
            def _():
                gather_in(s, xp).wait_recv()
                results[s][xp * qr:(xp + 1) * qr, :] = in_d[s, xp]

    last_pair = (remote(res_f, fin_f, sems.at[0, 1, 0, 0], sems.at[1, 1, 0, 0], (partner, head)),
                 remote(res_b, fin_b, sems.at[0, 1, 1, 0], sems.at[1, 1, 1, 0], (partner, head)))
    for copy in last_pair:
        copy.start()
    for copy in last_pair:
        copy.wait_recv()

    for mine in range(2):
        rows = pl.ds(mine * half, half)
        other = pl.ds((1 - mine) * half, half)

        @pl.when(core == mine)
        def _():
            if mine == 0:
                fwd_out[rows, :] = res_f[...]
                fwd_out[other, :] = fin_f[...]
                bwd_out[rows, :] = res_b[...] + peer_b[rows, :]
                bwd_out[other, :] = fin_b[...] + peer_b[other, :]
            else:
                fwd_out[rows, :] = res_f[...] + peer_f[rows, :]
                fwd_out[other, :] = fin_f[...] + peer_f[other, :]
                bwd_out[rows, :] = res_b[...]
                bwd_out[other, :] = fin_b[...]

    for h in range(heads):
        rows = slice(h * dim, (h + 1) * dim)
        running = fwd_out[rows, :]
        for n in range(nblocks):
            block_sum = kv_blk[n, rows, :]
            kv_blk[n, rows, :] = running
            if n + 1 < nblocks:
                running = running + block_sum
        running = bwd_out[rows, :]
        for n in reversed(range(nblocks)):
            block_sum = g_blk[n, rows, :]
            g_blk[n, rows, :] = running
            if n > 0:
                running = running + block_sum

    vm_out = (gq_ref, gk_ref, gv_ref)
    hbm_out = (gq_hbm, gk_hbm, gv_hbm)

    def gather_out(a, j):
        return pltpu.make_async_remote_copy(
            src_ref=vm_out[a].at[pl.ds(j * rows_in, rows_in)],
            dst_ref=hbm_out[a].at[:, pl.ds(head * cols_in, cols_in)],
            send_sem=x_sems.at[0, 4 + a, j], recv_sem=x_sems.at[1, 4 + a, head],
            device_id=(me, j), device_id_type=MESH)

    def gather_out_in(a, j):
        return pltpu.make_async_remote_copy(
            src_ref=vm_out[a].at[pl.ds(j * rows_in, rows_in)],
            dst_ref=hbm_out[a].at[:, pl.ds(j * cols_in, cols_in)],
            send_sem=x_sems.at[0, 4 + a, j], recv_sem=x_sems.at[1, 4 + a, j],
            device_id=(me, j), device_id_type=MESH)

    stores = [pltpu.make_async_copy(vm_out[a].at[pl.ds(head * rows_in, rows_in)],
                                    hbm_out[a].at[:, pl.ds(head * cols_in, cols_in)], io_sems.at[4 + a])
              for a in range(3)]
    per_block = blk // rows_in
    for n in range(nblocks):
        out_rows = slice(n * blk, (n + 1) * blk)
        for h in range(heads):
            rows = slice(h * dim, (h + 1) * dim)
            out_cols = slice(h * dim, (h + 1) * dim)
            kf = cut(k_ref, n, h).astype(jnp.float32)
            vf = cut(v_ref, n, h).astype(jnp.float32)
            df = cut(d_ref, n, h).astype(jnp.float32)
            kv_s = kv_blk[n, rows, :]
            g_s = g_blk[n, rows, :]
            gq_ref[out_rows, out_cols] = (
                scale * (acc_q[out_rows, out_cols] + _dot(df, kv_s, precise=True))
            ).astype(gq_ref.dtype)
            gk_ref[out_rows, out_cols] = (
                scale * (acc_k[out_rows, out_cols] + _dot(vf, g_s, precise=True))
            ).astype(gk_ref.dtype)
            gv_ref[out_rows, out_cols] = (
                acc_v[out_rows, out_cols] + scale * _dot(kf, g_s, tb=True, precise=True)
            ).astype(gv_ref.dtype)
        for j in range(n * per_block, (n + 1) * per_block):
            for a in range(3):
                @pl.when(head != j)
                def _():
                    gather_out(a, j).start()

                @pl.when(head == j)
                def _():
                    stores[a].start()

    for copy in first + last_pair:
        copy.wait_send()
    for s in range(2):
        for xp in range(plane):
            @pl.when(x != xp)
            def _():
                scatter(s, xp).wait_send()
                gather(s, xp).wait_send()
    for k in range(rounds):
        shift = 1 << k
        up, down = z_copies(k)

        @pl.when(z + shift < planes)
        def _():
            up.wait_send()

        @pl.when(z >= shift)
        def _():
            down.wait_send()
    for copy in stores:
        copy.wait()
    for a in range(4):
        for j in range(ways):
            @pl.when(head != j)
            def _():
                spread_in(a, j).wait_send()
    for a in range(3):
        for j in range(ways):
            @pl.when(head != j)
            def _():
                gather_out_in(a, j).wait_send()
                gather_out_in(a, j).wait_recv()


PLANE = 4
VMEM_ALL = 67043328


def core_math(q_rows, k_rows, v_rows, d_rows):
    count = lax.axis_size("ctx")
    ways = lax.axis_size("head")
    rows_in, full_width = q_rows.shape
    tokens, width = rows_in * ways, full_width // ways
    scale = (HEAD_DIM * tokens * count) ** (-0.5)
    chips = count // 2
    plane = PLANE if chips % PLANE == 0 else 1
    planes = chips // plane
    rounds = max(1, (planes - 1).bit_length())
    heads = width // HEAD_DIM
    nblocks = tokens // GROUP
    rows = heads * HEAD_DIM
    half = rows // 2
    qr = half // plane
    cols = HEAD_DIM
    anywhere = pl.BlockSpec(memory_space=pl.ANY)
    f32 = jnp.float32
    return pl.pallas_call(
        functools.partial(core_kernel, plane, planes, rounds, half, nblocks, heads, scale, ways),
        out_shape=(jax.ShapeDtypeStruct(q_rows.shape, q_rows.dtype),) * 3,
        in_specs=[anywhere] * 4,
        out_specs=(anywhere,) * 3,
        scratch_shapes=[
            *[pltpu.VMEM((tokens, width), q_rows.dtype) for _ in range(7)],
            pltpu.SemaphoreType.DMA((7,)),
            pltpu.VMEM((rows, cols), f32),
            pltpu.VMEM((rows, cols), f32),
            pltpu.VMEM((nblocks, rows, cols), f32),
            pltpu.VMEM((nblocks, rows, cols), f32),
            pltpu.VMEM((tokens, width), f32),
            pltpu.VMEM((tokens, width), f32),
            pltpu.VMEM((tokens, width), f32),
            pltpu.VMEM((rows, cols), f32),
            pltpu.VMEM((rows, cols), f32),
            pltpu.VMEM((half, cols), f32),
            pltpu.VMEM((half, cols), f32),
            pltpu.VMEM((2, plane, qr, cols), f32),
            pltpu.VMEM((2, plane, qr, cols), f32),
            pltpu.VMEM((rounds, qr, cols), f32),
            pltpu.VMEM((rounds, qr, cols), f32),
            pltpu.VMEM((rounds, qr, cols), f32),
            pltpu.VMEM((rounds, qr, cols), f32),
            pltpu.VMEM((qr, cols), f32),
            pltpu.VMEM((qr, cols), f32),
            pltpu.VMEM((2, plane, qr, cols), f32),
            pltpu.VMEM((2, plane, qr, cols), f32),
            pltpu.VMEM((half, cols), f32),
            pltpu.VMEM((half, cols), f32),
            pltpu.VMEM((half, cols), f32),
            pltpu.VMEM((half, cols), f32),
            pltpu.VMEM((rows, cols), f32),
            pltpu.VMEM((rows, cols), f32),
            pltpu.SemaphoreType.DMA((2, 5, 2, max(plane, rounds))),
            pltpu.SemaphoreType.DMA((2, 7, ways)),
        ],
        compiler_params=pltpu.CompilerParams(collective_id=0, has_side_effects=True,
                                             vmem_limit_bytes=VMEM_ALL),
    )(q_rows, k_rows, v_rows, d_rows)


def exchange_kernel(count, n_arrays, src_cut, dst_cut, *refs):
    srcs = refs[:n_arrays]
    dsts = refs[n_arrays:2 * n_arrays]
    send_sems, recv_sems, local_sems = refs[2 * n_arrays:]
    me = lax.axis_index("head")
    place = lax.axis_index("ctx")
    barrier = pltpu.get_barrier_semaphore()
    for j in range(count):
        @pl.when(me != j)
        def _():
            pl.semaphore_signal(barrier, inc=1, device_id=(place, j), device_id_type=MESH)
    pl.semaphore_wait(barrier, count - 1)

    def remote(a, j, dst_index):
        return pltpu.make_async_remote_copy(
            src_ref=src_cut(srcs[a], j), dst_ref=dst_cut(dsts[a], dst_index),
            send_sem=send_sems.at[a, j], recv_sem=recv_sems.at[a, me],
            device_id=(place, j), device_id_type=MESH)

    for a in range(n_arrays):
        local = pltpu.make_async_copy(src_cut(srcs[a], me), dst_cut(dsts[a], me), local_sems.at[a])
        local.start()
    for step in range(1, count):
        for a in range(n_arrays):
            j_dyn = lax.rem(me + step, count)
            for j in range(count):
                @pl.when(j_dyn == j)
                def _():
                    remote(a, j, me).start()
    for a in range(n_arrays):
        pltpu.make_async_copy(src_cut(srcs[a], me), dst_cut(dsts[a], me), local_sems.at[a]).wait()
    for a in range(n_arrays):
        for j in range(count):
            @pl.when(me != j)
            def _():
                copy = pltpu.make_async_remote_copy(
                    src_ref=src_cut(srcs[a], j), dst_ref=dst_cut(dsts[a], j),
                    send_sem=send_sems.at[a, j], recv_sem=recv_sems.at[a, j],
                    device_id=(place, j), device_id_type=MESH)
                copy.wait_send()
                copy.wait_recv()


def exchange(arrays, out_shape, src_cut, dst_cut, collective_id, in_space, out_space):
    count = lax.axis_size("head")
    if count == 1:
        return tuple(arrays)
    n_arrays = len(arrays)
    in_spec = pl.BlockSpec(memory_space=in_space)
    out_spec = pl.BlockSpec(memory_space=out_space)
    return pl.pallas_call(
        functools.partial(exchange_kernel, count, n_arrays, src_cut, dst_cut),
        out_shape=tuple(jax.ShapeDtypeStruct(out_shape, arrays[0].dtype) for _ in arrays),
        in_specs=[in_spec] * n_arrays,
        out_specs=tuple(out_spec for _ in arrays),
        scratch_shapes=[
            pltpu.SemaphoreType.DMA((n_arrays, count)),
            pltpu.SemaphoreType.DMA((n_arrays, count)),
            pltpu.SemaphoreType.DMA((n_arrays,)),
        ],
        compiler_params=pltpu.CompilerParams(collective_id=collective_id, has_side_effects=True,
                                             vmem_limit_bytes=VMEM_ALL),
    )(*arrays)


def per_device(queries, key_rows, value_rows, grad_out):
    return core_math(queries, key_rows, value_rows, grad_out)


def solution(mesh):
    placed = (
        P(("ctx", "head"), None),
        P(("ctx", "head"), None),
        P(("ctx", "head"), None),
        P(("ctx", "head"), None),
    )
    return jax.shard_map(
        per_device,
        mesh=mesh,
        in_specs=placed,
        out_specs=(P(("ctx", "head"), None), P(("ctx", "head"), None), P(("ctx", "head"), None)),
        check_vma=False,
    )
```

```python
import functools

import jax
import jax.numpy as jnp
from jax import lax
from jax.experimental import pallas as pl
from jax.experimental.pallas import tpu as pltpu
from jax.sharding import PartitionSpec as P

HEAD_DIM = 128
GROUP = 128


MESH = pl.DeviceIdType.MESH


def _dot(a, b, ta=False, tb=False, precise=False):
    dims = (((0 if ta else 1,), (1 if tb else 0,)), ((), ()))
    return lax.dot_general(a, b, dims, preferred_element_type=jnp.float32,
                           precision=lax.Precision.HIGHEST if precise else None)


def core_kernel(plane, planes, rounds, stages, nblocks, heads, scale, ways,
                q_hbm, k_hbm, v_hbm, d_hbm, gq_hbm, gk_hbm, gv_hbm,
                q_ref, k_ref, v_ref, d_ref, gq_ref, gk_ref, gv_ref, io_sems,
                fwd_in, bwd_in, kv_blk, g_blk, acc_q, acc_k, acc_v,
                peer_f, peer_b, th_f, th_b, in_b1, pre, tz_f, tz_b, got_f, got_b,
                ez_f, ez_b, out_d, in_d, res_f, res_b, fin_f, fin_b,
                fwd_out, bwd_out, sems, x_sems):
    me = lax.axis_index("ctx")
    head = lax.axis_index("head")
    core = lax.rem(me, 2)
    chip = me // 2
    x = lax.rem(chip, plane)
    z = chip // plane
    partner = me + 1 - 2 * core
    blk = GROUP
    dim = HEAD_DIM
    hs = heads // stages
    rows_s = hs * dim
    half = rows_s // 2
    qr = half // plane
    rows_in = q_hbm.shape[0]
    cols_in = q_ref.shape[1]
    cols_s = hs * dim

    def dev(xp, zp):
        return ((zp * plane + xp) * 2 + core, head)

    barrier = pltpu.get_barrier_semaphore()
    pl.semaphore_signal(barrier, inc=1, device_id=(partner, head), device_id_type=MESH)
    peers = 1
    for xp in range(plane):
        @pl.when(x != xp)
        def _():
            pl.semaphore_signal(barrier, inc=1, device_id=dev(xp, z), device_id_type=MESH)

        peers = peers + (x != xp).astype(jnp.int32)
    for k in range(rounds):
        shift = 1 << k

        @pl.when(z + shift < planes)
        def _():
            pl.semaphore_signal(barrier, inc=1, device_id=dev(x, z + shift), device_id_type=MESH)

        @pl.when(z >= shift)
        def _():
            pl.semaphore_signal(barrier, inc=1, device_id=dev(x, z - shift), device_id_type=MESH)

        peers = peers + (z + shift < planes).astype(jnp.int32) + (z >= shift).astype(jnp.int32)
    for j in range(ways):
        @pl.when(head != j)
        def _():
            pl.semaphore_signal(barrier, inc=1, device_id=(me, j), device_id_type=MESH)
    pl.semaphore_wait(barrier, peers + (ways - 1))

    hbm_in = (q_hbm, k_hbm, v_hbm, d_hbm)
    vm_in = (q_ref, k_ref, v_ref, d_ref)
    vm_out = (gq_ref, gk_ref, gv_ref)
    hbm_out = (gq_hbm, gk_hbm, gv_hbm)

    def spread(st, a, j, slot):
        return pltpu.make_async_remote_copy(
            src_ref=hbm_in[a].at[:, pl.ds(j * cols_in + st * cols_s, cols_s)],
            dst_ref=vm_in[a].at[pl.ds(slot * rows_in, rows_in), pl.ds(st * cols_s, cols_s)],
            send_sem=x_sems.at[st, 0, a, j], recv_sem=x_sems.at[st, 1, a, slot],
            device_id=(me, j), device_id_type=MESH)

    def spread_in(st, a, j):
        return spread(st, a, j, j)

    def load(st, a):
        return pltpu.make_async_copy(
            hbm_in[a].at[:, pl.ds(head * cols_in + st * cols_s, cols_s)],
            vm_in[a].at[pl.ds(head * rows_in, rows_in), pl.ds(st * cols_s, cols_s)],
            io_sems.at[st, a])

    def gather_out(st, a, j, slot):
        return pltpu.make_async_remote_copy(
            src_ref=vm_out[a].at[pl.ds(j * rows_in, rows_in), pl.ds(st * cols_s, cols_s)],
            dst_ref=hbm_out[a].at[:, pl.ds(slot * cols_in + st * cols_s, cols_s)],
            send_sem=x_sems.at[st, 0, 4 + a, j], recv_sem=x_sems.at[st, 1, 4 + a, slot],
            device_id=(me, j), device_id_type=MESH)

    def store(st, a):
        return pltpu.make_async_copy(
            vm_out[a].at[pl.ds(head * rows_in, rows_in), pl.ds(st * cols_s, cols_s)],
            hbm_out[a].at[:, pl.ds(head * cols_in + st * cols_s, cols_s)],
            io_sems.at[st, 4 + a])

    for st in range(stages):
        for step in range(1, ways):
            for a in range(4):
                j_dyn = lax.rem(head + step, ways)
                for j in range(ways):
                    @pl.when(j_dyn == j)
                    def _():
                        spread(st, a, j, head).start()
        for a in range(4):
            load(st, a).start()

    def cut(ref, n, h):
        return ref[n * blk:(n + 1) * blk, h * dim:(h + 1) * dim]

    def remote(src, dst, sem_send, sem_recv, device):
        return pltpu.make_async_remote_copy(
            src_ref=src, dst_ref=dst, send_sem=sem_send, recv_sem=sem_recv,
            device_id=device, device_id_type=MESH)

    later = lax.broadcasted_iota(jnp.int32, (blk, blk), 0)
    earlier = lax.broadcasted_iota(jnp.int32, (blk, blk), 1)
    causal = later >= earlier
    per_block = blk // rows_in

    def stage_copies(st):
        sm = sems.at[st]
        fi, bi = fwd_in.at[st], bwd_in.at[st]
        pf, pb = peer_f.at[st], peer_b.at[st]
        first = (remote(fi, pf, sm.at[0, 0, 0, 0], sm.at[1, 0, 0, 0], (partner, head)),
                 remote(bi, pb, sm.at[0, 0, 1, 0], sm.at[1, 0, 1, 0], (partner, head)))
        halves = (th_f.at[st], th_b.at[st])
        inb = in_b1.at[st]

        def scatter(s, xp):
            return remote(halves[s].at[pl.ds(xp * qr, qr)], inb.at[s, x],
                          sm.at[0, 2, s, xp], sm.at[1, 2, s, x], dev(xp, z))

        def scatter_in(s, xp):
            return remote(halves[s].at[pl.ds(xp * qr, qr)], inb.at[s, xp],
                          sm.at[0, 2, s, xp], sm.at[1, 2, s, xp], dev(xp, z))

        def z_copies(k):
            shift = 1 << k
            up = remote(tz_f.at[st, k], got_f.at[st, k], sm.at[0, 3, 0, k], sm.at[1, 3, 0, k],
                        dev(x, z + shift))
            down = remote(tz_b.at[st, k], got_b.at[st, k], sm.at[0, 3, 1, k], sm.at[1, 3, 1, k],
                          dev(x, z - shift))
            return up, down

        od, idd = out_d.at[st], in_d.at[st]

        def gather(s, xp):
            return remote(od.at[s, xp], idd.at[s, x], sm.at[0, 4, s, xp], sm.at[1, 4, s, x], dev(xp, z))

        def gather_in(s, xp):
            return remote(od.at[s, xp], idd.at[s, xp], sm.at[0, 4, s, xp], sm.at[1, 4, s, xp], dev(xp, z))

        last_pair = (remote(res_f.at[st], fin_f.at[st], sm.at[0, 1, 0, 0], sm.at[1, 1, 0, 0], (partner, head)),
                     remote(res_b.at[st], fin_b.at[st], sm.at[0, 1, 1, 0], sm.at[1, 1, 1, 0], (partner, head)))
        return first, scatter, scatter_in, z_copies, gather, gather_in, last_pair

    for st in range(stages):
        first, scatter, scatter_in, z_copies, gather, gather_in, last_pair = stage_copies(st)
        for a in range(4):
            load(st, a).wait()
            for j in range(ways):
                @pl.when(head != j)
                def _():
                    spread_in(st, a, j).wait_recv()

        for hh in range(hs):
            h = st * hs + hh
            rows = slice(hh * dim, (hh + 1) * dim)
            for n in range(nblocks):
                kv_blk[n, h * dim:(h + 1) * dim, :] = _dot(cut(v_ref, n, h), cut(k_ref, n, h), ta=True)
                g_blk[n, h * dim:(h + 1) * dim, :] = _dot(cut(d_ref, n, h), cut(q_ref, n, h), ta=True)
            kv_sum = kv_blk[0, h * dim:(h + 1) * dim, :]
            g_sum = g_blk[0, h * dim:(h + 1) * dim, :]
            for n in range(1, nblocks):
                kv_sum = kv_sum + kv_blk[n, h * dim:(h + 1) * dim, :]
                g_sum = g_sum + g_blk[n, h * dim:(h + 1) * dim, :]
            fwd_in[st, rows, :] = kv_sum
            bwd_in[st, rows, :] = g_sum

        for copy in first:
            copy.start()

        for hh in range(hs):
            h = st * hs + hh
            for n in range(nblocks):
                qb, kb, vb, db = (cut(r, n, h) for r in (q_ref, k_ref, v_ref, d_ref))
                scores = jnp.where(causal, _dot(qb, kb, tb=True) * scale, 0.0).astype(jnp.bfloat16)
                dscores = jnp.where(causal, _dot(db, vb, tb=True), 0.0).astype(jnp.bfloat16)
                out_rows = slice(n * blk, (n + 1) * blk)
                out_cols = slice(h * dim, (h + 1) * dim)
                acc_q[out_rows, out_cols] = _dot(dscores, kb)
                acc_k[out_rows, out_cols] = _dot(dscores, qb, ta=True)
                acc_v[out_rows, out_cols] = _dot(scores, db, ta=True)

        for copy in first:
            copy.wait_recv()

        for mine in range(2):
            rows = pl.ds(mine * half, half)

            @pl.when(core == mine)
            def _():
                th_f[st] = fwd_in[st, rows, :] + peer_f[st, rows, :]
                th_b[st] = bwd_in[st, rows, :] + peer_b[st, rows, :]

        halves = (th_f.at[st], th_b.at[st])
        for s in range(2):
            for xp in range(plane):
                @pl.when(x != xp)
                def _():
                    scatter(s, xp).start()
        for s in range(2):
            in_b1[st, s, x] = halves[s][pl.ds(x * qr, qr), :]
        for s in range(2):
            for xp in range(plane):
                @pl.when(x != xp)
                def _():
                    scatter_in(s, xp).wait_recv()

        run = jnp.zeros((qr, dim), jnp.float32)
        for xp in range(plane):
            pre[st, 0, xp] = run
            run = run + in_b1[st, 0, xp]
        tz_f[st, 0] = run
        run = jnp.zeros((qr, dim), jnp.float32)
        for xp in reversed(range(plane)):
            pre[st, 1, xp] = run
            run = run + in_b1[st, 1, xp]
        tz_b[st, 0] = run

        ez_f[st] = jnp.zeros((qr, dim), jnp.float32)
        ez_b[st] = jnp.zeros((qr, dim), jnp.float32)

        for k in range(rounds):
            shift = 1 << k
            up, down = z_copies(k)
            last = k == rounds - 1

            @pl.when(z + shift < planes)
            def _():
                up.start()

            @pl.when(z >= shift)
            def _():
                down.start()

            @pl.when(z >= shift)
            def _():
                up.wait_recv()
                got = got_f[st, k]
                ez_f[st] = ez_f[st] + got
                if not last:
                    tz_f[st, k + 1] = tz_f[st, k] + got

            @pl.when(z < shift)
            def _():
                if not last:
                    tz_f[st, k + 1] = tz_f[st, k]

            @pl.when(z + shift < planes)
            def _():
                down.wait_recv()
                got = got_b[st, k]
                ez_b[st] = ez_b[st] + got
                if not last:
                    tz_b[st, k + 1] = tz_b[st, k] + got

            @pl.when(z + shift >= planes)
            def _():
                if not last:
                    tz_b[st, k + 1] = tz_b[st, k]

        zs = (ez_f, ez_b)
        for s in range(2):
            for xp in range(plane):
                out_d[st, s, xp] = zs[s][st] + pre[st, s, xp]
        for s in range(2):
            for xp in range(plane):
                @pl.when(x != xp)
                def _():
                    gather(s, xp).start()
        results = (res_f, res_b)
        for s in range(2):
            results[s][st, pl.ds(x * qr, qr), :] = out_d[st, s, x]
        for s in range(2):
            for xp in range(plane):
                @pl.when(x != xp)
                def _():
                    gather_in(s, xp).wait_recv()
                    results[s][st, xp * qr:(xp + 1) * qr, :] = in_d[st, s, xp]

        for copy in last_pair:
            copy.start()
        for copy in last_pair:
            copy.wait_recv()

        for mine in range(2):
            rows = pl.ds(mine * half, half)
            other = pl.ds((1 - mine) * half, half)

            @pl.when(core == mine)
            def _():
                if mine == 0:
                    fwd_out[st, rows, :] = res_f[st]
                    fwd_out[st, other, :] = fin_f[st]
                    bwd_out[st, rows, :] = res_b[st] + peer_b[st, rows, :]
                    bwd_out[st, other, :] = fin_b[st] + peer_b[st, other, :]
                else:
                    fwd_out[st, rows, :] = res_f[st] + peer_f[st, rows, :]
                    fwd_out[st, other, :] = fin_f[st] + peer_f[st, other, :]
                    bwd_out[st, rows, :] = res_b[st]
                    bwd_out[st, other, :] = fin_b[st]

        for hh in range(hs):
            h = st * hs + hh
            srows = slice(hh * dim, (hh + 1) * dim)
            hrows = slice(h * dim, (h + 1) * dim)
            running = fwd_out[st, srows, :]
            for n in range(nblocks):
                block_sum = kv_blk[n, hrows, :]
                kv_blk[n, hrows, :] = running
                if n + 1 < nblocks:
                    running = running + block_sum
            running = bwd_out[st, srows, :]
            for n in reversed(range(nblocks)):
                block_sum = g_blk[n, hrows, :]
                g_blk[n, hrows, :] = running
                if n > 0:
                    running = running + block_sum

        for n in range(nblocks):
            out_rows = slice(n * blk, (n + 1) * blk)
            for hh in range(hs):
                h = st * hs + hh
                hrows = slice(h * dim, (h + 1) * dim)
                out_cols = slice(h * dim, (h + 1) * dim)
                kf = cut(k_ref, n, h).astype(jnp.float32)
                vf = cut(v_ref, n, h).astype(jnp.float32)
                df = cut(d_ref, n, h).astype(jnp.float32)
                kv_s = kv_blk[n, hrows, :]
                g_s = g_blk[n, hrows, :]
                gq_ref[out_rows, out_cols] = (
                    scale * (acc_q[out_rows, out_cols] + _dot(df, kv_s, precise=True))
                ).astype(gq_ref.dtype)
                gk_ref[out_rows, out_cols] = (
                    scale * (acc_k[out_rows, out_cols] + _dot(vf, g_s, precise=True))
                ).astype(gk_ref.dtype)
                gv_ref[out_rows, out_cols] = (
                    acc_v[out_rows, out_cols] + scale * _dot(kf, g_s, tb=True, precise=True)
                ).astype(gv_ref.dtype)
            for j in range(n * per_block, (n + 1) * per_block):
                for a in range(3):
                    @pl.when(head != j)
                    def _():
                        gather_out(st, a, j, head).start()

                    @pl.when(head == j)
                    def _():
                        store(st, a).start()

    for st in range(stages):
        first, scatter, scatter_in, z_copies, gather, gather_in, last_pair = stage_copies(st)
        for copy in first + last_pair:
            copy.wait_send()
        for s in range(2):
            for xp in range(plane):
                @pl.when(x != xp)
                def _():
                    scatter(s, xp).wait_send()
                    gather(s, xp).wait_send()
        for k in range(rounds):
            shift = 1 << k
            up, down = z_copies(k)

            @pl.when(z + shift < planes)
            def _():
                up.wait_send()

            @pl.when(z >= shift)
            def _():
                down.wait_send()
        for a in range(3):
            store(st, a).wait()
        for a in range(4):
            for j in range(ways):
                @pl.when(head != j)
                def _():
                    spread_in(st, a, j).wait_send()
        for a in range(3):
            for j in range(ways):
                @pl.when(head != j)
                def _():
                    gather_out(st, a, j, j).wait_send()
                    gather_out(st, a, j, j).wait_recv()


PLANE = 4
VMEM_ALL = 67043328
STAGES = 2


def core_math(q_rows, k_rows, v_rows, d_rows):
    count = lax.axis_size("ctx")
    ways = lax.axis_size("head")
    rows_in, full_width = q_rows.shape
    tokens, width = rows_in * ways, full_width // ways
    scale = (HEAD_DIM * tokens * count) ** (-0.5)
    chips = count // 2
    plane = PLANE if chips % PLANE == 0 else 1
    planes = chips // plane
    rounds = max(1, (planes - 1).bit_length())
    heads = width // HEAD_DIM
    stages = STAGES if heads % STAGES == 0 else 1
    nblocks = tokens // GROUP
    rows = heads * HEAD_DIM
    rows_s = rows // stages
    half = rows_s // 2
    qr = half // plane
    cols = HEAD_DIM
    anywhere = pl.BlockSpec(memory_space=pl.ANY)
    f32 = jnp.float32
    return pl.pallas_call(
        functools.partial(core_kernel, plane, planes, rounds, stages, nblocks, heads, scale, ways),
        out_shape=(jax.ShapeDtypeStruct(q_rows.shape, q_rows.dtype),) * 3,
        in_specs=[anywhere] * 4,
        out_specs=(anywhere,) * 3,
        scratch_shapes=[
            *[pltpu.VMEM((tokens, width), q_rows.dtype) for _ in range(7)],
            pltpu.SemaphoreType.DMA((stages, 7)),
            pltpu.VMEM((stages, rows_s, cols), f32),
            pltpu.VMEM((stages, rows_s, cols), f32),
            pltpu.VMEM((nblocks, rows, cols), f32),
            pltpu.VMEM((nblocks, rows, cols), f32),
            pltpu.VMEM((tokens, width), f32),
            pltpu.VMEM((tokens, width), f32),
            pltpu.VMEM((tokens, width), f32),
            pltpu.VMEM((stages, rows_s, cols), f32),
            pltpu.VMEM((stages, rows_s, cols), f32),
            pltpu.VMEM((stages, half, cols), f32),
            pltpu.VMEM((stages, half, cols), f32),
            pltpu.VMEM((stages, 2, plane, qr, cols), f32),
            pltpu.VMEM((stages, 2, plane, qr, cols), f32),
            pltpu.VMEM((stages, rounds, qr, cols), f32),
            pltpu.VMEM((stages, rounds, qr, cols), f32),
            pltpu.VMEM((stages, rounds, qr, cols), f32),
            pltpu.VMEM((stages, rounds, qr, cols), f32),
            pltpu.VMEM((stages, qr, cols), f32),
            pltpu.VMEM((stages, qr, cols), f32),
            pltpu.VMEM((stages, 2, plane, qr, cols), f32),
            pltpu.VMEM((stages, 2, plane, qr, cols), f32),
            pltpu.VMEM((stages, half, cols), f32),
            pltpu.VMEM((stages, half, cols), f32),
            pltpu.VMEM((stages, half, cols), f32),
            pltpu.VMEM((stages, half, cols), f32),
            pltpu.VMEM((stages, rows_s, cols), f32),
            pltpu.VMEM((stages, rows_s, cols), f32),
            pltpu.SemaphoreType.DMA((stages, 2, 5, 2, max(plane, rounds))),
            pltpu.SemaphoreType.DMA((stages, 2, 7, ways)),
        ],
        compiler_params=pltpu.CompilerParams(collective_id=0, has_side_effects=True,
                                             vmem_limit_bytes=VMEM_ALL),
    )(q_rows, k_rows, v_rows, d_rows)


def exchange_kernel(count, n_arrays, src_cut, dst_cut, *refs):
    srcs = refs[:n_arrays]
    dsts = refs[n_arrays:2 * n_arrays]
    send_sems, recv_sems, local_sems = refs[2 * n_arrays:]
    me = lax.axis_index("head")
    place = lax.axis_index("ctx")
    barrier = pltpu.get_barrier_semaphore()
    for j in range(count):
        @pl.when(me != j)
        def _():
            pl.semaphore_signal(barrier, inc=1, device_id=(place, j), device_id_type=MESH)
    pl.semaphore_wait(barrier, count - 1)

    def remote(a, j, dst_index):
        return pltpu.make_async_remote_copy(
            src_ref=src_cut(srcs[a], j), dst_ref=dst_cut(dsts[a], dst_index),
            send_sem=send_sems.at[a, j], recv_sem=recv_sems.at[a, me],
            device_id=(place, j), device_id_type=MESH)

    for a in range(n_arrays):
        local = pltpu.make_async_copy(src_cut(srcs[a], me), dst_cut(dsts[a], me), local_sems.at[a])
        local.start()
    for step in range(1, count):
        for a in range(n_arrays):
            j_dyn = lax.rem(me + step, count)
            for j in range(count):
                @pl.when(j_dyn == j)
                def _():
                    remote(a, j, me).start()
    for a in range(n_arrays):
        pltpu.make_async_copy(src_cut(srcs[a], me), dst_cut(dsts[a], me), local_sems.at[a]).wait()
    for a in range(n_arrays):
        for j in range(count):
            @pl.when(me != j)
            def _():
                copy = pltpu.make_async_remote_copy(
                    src_ref=src_cut(srcs[a], j), dst_ref=dst_cut(dsts[a], j),
                    send_sem=send_sems.at[a, j], recv_sem=recv_sems.at[a, j],
                    device_id=(place, j), device_id_type=MESH)
                copy.wait_send()
                copy.wait_recv()


def exchange(arrays, out_shape, src_cut, dst_cut, collective_id, in_space, out_space):
    count = lax.axis_size("head")
    if count == 1:
        return tuple(arrays)
    n_arrays = len(arrays)
    in_spec = pl.BlockSpec(memory_space=in_space)
    out_spec = pl.BlockSpec(memory_space=out_space)
    return pl.pallas_call(
        functools.partial(exchange_kernel, count, n_arrays, src_cut, dst_cut),
        out_shape=tuple(jax.ShapeDtypeStruct(out_shape, arrays[0].dtype) for _ in arrays),
        in_specs=[in_spec] * n_arrays,
        out_specs=tuple(out_spec for _ in arrays),
        scratch_shapes=[
            pltpu.SemaphoreType.DMA((n_arrays, count)),
            pltpu.SemaphoreType.DMA((n_arrays, count)),
            pltpu.SemaphoreType.DMA((n_arrays,)),
        ],
        compiler_params=pltpu.CompilerParams(collective_id=collective_id, has_side_effects=True,
                                             vmem_limit_bytes=VMEM_ALL),
    )(*arrays)


def per_device(queries, key_rows, value_rows, grad_out):
    return core_math(queries, key_rows, value_rows, grad_out)


def solution(mesh):
    placed = (
        P(("ctx", "head"), None),
        P(("ctx", "head"), None),
        P(("ctx", "head"), None),
        P(("ctx", "head"), None),
    )
    return jax.shard_map(
        per_device,
        mesh=mesh,
        in_specs=placed,
        out_specs=(P(("ctx", "head"), None), P(("ctx", "head"), None), P(("ctx", "head"), None)),
        check_vma=False,
    )
```

```python
import functools

import jax
import jax.numpy as jnp
from jax import lax
from jax.experimental import pallas as pl
from jax.experimental.pallas import tpu as pltpu
from jax.sharding import PartitionSpec as P

HEAD_DIM = 128
GROUP = 128


MESH = pl.DeviceIdType.MESH


def _dot(a, b, ta=False, tb=False, precise=False):
    dims = (((0 if ta else 1,), (1 if tb else 0,)), ((), ()))
    return lax.dot_general(a, b, dims, preferred_element_type=jnp.float32,
                           precision=lax.Precision.HIGHEST if precise else None)


def _split_dot(a, b, tb=False):
    hi = b.astype(jnp.bfloat16)
    lo = (b - hi.astype(jnp.float32)).astype(jnp.bfloat16)
    return _dot(a, hi, tb=tb) + _dot(a, lo, tb=tb)


def core_kernel(plane, planes, rounds, half, nblocks, heads, scale, ways,
                q_hbm, k_hbm, v_hbm, d_hbm, gq_hbm, gk_hbm, gv_hbm,
                q_ref, k_ref, v_ref, d_ref, gq_ref, gk_ref, gv_ref, io_sems,
                fwd_in, bwd_in, kv_blk, g_blk, acc_q, acc_k, acc_v,
                peer_f, peer_b, th_f, th_b, in_b1, pre, tz_f, tz_b, got_f, got_b,
                ez_f, ez_b, out_d, in_d, res_f, res_b, fin_f, fin_b,
                fwd_out, bwd_out, sems, x_sems):
    me = lax.axis_index("ctx")
    head = lax.axis_index("head")
    core = lax.rem(me, 2)
    chip = me // 2
    x = lax.rem(chip, plane)
    z = chip // plane
    partner = me + 1 - 2 * core
    qr = half // plane

    def dev(xp, zp):
        return ((zp * plane + xp) * 2 + core, head)

    barrier = pltpu.get_barrier_semaphore()
    pl.semaphore_signal(barrier, inc=1, device_id=(partner, head), device_id_type=MESH)
    peers = 1
    for xp in range(plane):
        @pl.when(x != xp)
        def _():
            pl.semaphore_signal(barrier, inc=1, device_id=dev(xp, z), device_id_type=MESH)

        peers = peers + (x != xp).astype(jnp.int32)
    for k in range(rounds):
        shift = 1 << k

        @pl.when(z + shift < planes)
        def _():
            pl.semaphore_signal(barrier, inc=1, device_id=dev(x, z + shift), device_id_type=MESH)

        @pl.when(z >= shift)
        def _():
            pl.semaphore_signal(barrier, inc=1, device_id=dev(x, z - shift), device_id_type=MESH)

        peers = peers + (z + shift < planes).astype(jnp.int32) + (z >= shift).astype(jnp.int32)
    for j in range(ways):
        @pl.when(head != j)
        def _():
            pl.semaphore_signal(barrier, inc=1, device_id=(me, j), device_id_type=MESH)
    pl.semaphore_wait(barrier, peers + (ways - 1))

    rows_in = q_hbm.shape[0]
    cols_in = q_ref.shape[1]
    hbm_in = (q_hbm, k_hbm, v_hbm, d_hbm)
    vm_in = (q_ref, k_ref, v_ref, d_ref)

    def spread(a, j):
        return pltpu.make_async_remote_copy(
            src_ref=hbm_in[a].at[:, pl.ds(j * cols_in, cols_in)],
            dst_ref=vm_in[a].at[pl.ds(head * rows_in, rows_in)],
            send_sem=x_sems.at[0, a, j], recv_sem=x_sems.at[1, a, head],
            device_id=(me, j), device_id_type=MESH)

    def spread_in(a, j):
        return pltpu.make_async_remote_copy(
            src_ref=hbm_in[a].at[:, pl.ds(j * cols_in, cols_in)],
            dst_ref=vm_in[a].at[pl.ds(j * rows_in, rows_in)],
            send_sem=x_sems.at[0, a, j], recv_sem=x_sems.at[1, a, j],
            device_id=(me, j), device_id_type=MESH)

    loads = [pltpu.make_async_copy(hbm_in[a].at[:, pl.ds(head * cols_in, cols_in)],
                                   vm_in[a].at[pl.ds(head * rows_in, rows_in)], io_sems.at[a])
             for a in range(4)]
    for step in range(1, ways):
        for a in range(4):
            j_dyn = lax.rem(head + step, ways)
            for j in range(ways):
                @pl.when(j_dyn == j)
                def _():
                    spread(a, j).start()
    for copy in loads:
        copy.start()
    for copy in loads:
        copy.wait()
    for a in range(4):
        for j in range(ways):
            @pl.when(head != j)
            def _():
                spread_in(a, j).wait_recv()

    blk = GROUP
    dim = HEAD_DIM

    def cut(ref, n, h):
        return ref[n * blk:(n + 1) * blk, h * dim:(h + 1) * dim]

    for h in range(heads):
        rows = slice(h * dim, (h + 1) * dim)
        for n in range(nblocks):
            kv_blk[n, rows, :] = _dot(cut(v_ref, n, h), cut(k_ref, n, h), ta=True)
            g_blk[n, rows, :] = _dot(cut(d_ref, n, h), cut(q_ref, n, h), ta=True)
        kv_sum = kv_blk[0, rows, :]
        g_sum = g_blk[0, rows, :]
        for n in range(1, nblocks):
            kv_sum = kv_sum + kv_blk[n, rows, :]
            g_sum = g_sum + g_blk[n, rows, :]
        fwd_in[rows, :] = kv_sum
        bwd_in[rows, :] = g_sum


    def remote(src, dst, sem_send, sem_recv, device):
        return pltpu.make_async_remote_copy(
            src_ref=src, dst_ref=dst, send_sem=sem_send, recv_sem=sem_recv,
            device_id=device, device_id_type=MESH)

    first = (remote(fwd_in, peer_f, sems.at[0, 0, 0, 0], sems.at[1, 0, 0, 0], (partner, head)),
             remote(bwd_in, peer_b, sems.at[0, 0, 1, 0], sems.at[1, 0, 1, 0], (partner, head)))
    for copy in first:
        copy.start()

    later = lax.broadcasted_iota(jnp.int32, (blk, blk), 0)
    earlier = lax.broadcasted_iota(jnp.int32, (blk, blk), 1)
    causal = later >= earlier
    for h in range(heads):
        for n in range(nblocks):
            qb, kb, vb, db = (cut(r, n, h) for r in (q_ref, k_ref, v_ref, d_ref))
            scores = jnp.where(causal, _dot(qb, kb, tb=True) * scale, 0.0).astype(jnp.bfloat16)
            dscores = jnp.where(causal, _dot(db, vb, tb=True), 0.0).astype(jnp.bfloat16)
            out_rows = slice(n * blk, (n + 1) * blk)
            out_cols = slice(h * dim, (h + 1) * dim)
            acc_q[out_rows, out_cols] = _dot(dscores, kb)
            acc_k[out_rows, out_cols] = _dot(dscores, qb, ta=True)
            acc_v[out_rows, out_cols] = _dot(scores, db, ta=True)

    for copy in first:
        copy.wait_recv()

    for mine in range(2):
        rows = pl.ds(mine * half, half)

        @pl.when(core == mine)
        def _():
            th_f[...] = fwd_in[rows, :] + peer_f[rows, :]
            th_b[...] = bwd_in[rows, :] + peer_b[rows, :]

    halves = (th_f, th_b)

    def scatter(s, xp):
        return remote(halves[s].at[pl.ds(xp * qr, qr)], in_b1.at[s, x],
                      sems.at[0, 2, s, xp], sems.at[1, 2, s, x], dev(xp, z))

    def scatter_in(s, xp):
        return remote(halves[s].at[pl.ds(xp * qr, qr)], in_b1.at[s, xp],
                      sems.at[0, 2, s, xp], sems.at[1, 2, s, xp], dev(xp, z))

    for s in range(2):
        for xp in range(plane):
            @pl.when(x != xp)
            def _():
                scatter(s, xp).start()
    for s in range(2):
        in_b1[s, x] = halves[s][pl.ds(x * qr, qr), :]
    for s in range(2):
        for xp in range(plane):
            @pl.when(x != xp)
            def _():
                scatter_in(s, xp).wait_recv()

    run = jnp.zeros((qr, HEAD_DIM), jnp.float32)
    for xp in range(plane):
        pre[0, xp] = run
        run = run + in_b1[0, xp]
    tz_f[0] = run
    run = jnp.zeros((qr, HEAD_DIM), jnp.float32)
    for xp in reversed(range(plane)):
        pre[1, xp] = run
        run = run + in_b1[1, xp]
    tz_b[0] = run

    ez_f[...] = jnp.zeros_like(ez_f)
    ez_b[...] = jnp.zeros_like(ez_b)

    def z_copies(k):
        shift = 1 << k
        up = remote(tz_f.at[k], got_f.at[k], sems.at[0, 3, 0, k], sems.at[1, 3, 0, k], dev(x, z + shift))
        down = remote(tz_b.at[k], got_b.at[k], sems.at[0, 3, 1, k], sems.at[1, 3, 1, k], dev(x, z - shift))
        return up, down

    for k in range(rounds):
        shift = 1 << k
        up, down = z_copies(k)
        last = k == rounds - 1

        @pl.when(z + shift < planes)
        def _():
            up.start()

        @pl.when(z >= shift)
        def _():
            down.start()

        @pl.when(z >= shift)
        def _():
            up.wait_recv()
            got = got_f[k]
            ez_f[...] += got
            if not last:
                tz_f[k + 1] = tz_f[k] + got

        @pl.when(z < shift)
        def _():
            if not last:
                tz_f[k + 1] = tz_f[k]

        @pl.when(z + shift < planes)
        def _():
            down.wait_recv()
            got = got_b[k]
            ez_b[...] += got
            if not last:
                tz_b[k + 1] = tz_b[k] + got

        @pl.when(z + shift >= planes)
        def _():
            if not last:
                tz_b[k + 1] = tz_b[k]

    zs = (ez_f, ez_b)
    for s in range(2):
        for xp in range(plane):
            out_d[s, xp] = zs[s][...] + pre[s, xp]

    def gather(s, xp):
        return remote(out_d.at[s, xp], in_d.at[s, x],
                      sems.at[0, 4, s, xp], sems.at[1, 4, s, x], dev(xp, z))

    def gather_in(s, xp):
        return remote(out_d.at[s, xp], in_d.at[s, xp],
                      sems.at[0, 4, s, xp], sems.at[1, 4, s, xp], dev(xp, z))

    for s in range(2):
        for xp in range(plane):
            @pl.when(x != xp)
            def _():
                gather(s, xp).start()
    results = (res_f, res_b)
    for s in range(2):
        results[s][pl.ds(x * qr, qr), :] = out_d[s, x]
    for s in range(2):
        for xp in range(plane):
            @pl.when(x != xp)
            def _():
                gather_in(s, xp).wait_recv()
                results[s][xp * qr:(xp + 1) * qr, :] = in_d[s, xp]

    last_pair = (remote(res_f, fin_f, sems.at[0, 1, 0, 0], sems.at[1, 1, 0, 0], (partner, head)),
                 remote(res_b, fin_b, sems.at[0, 1, 1, 0], sems.at[1, 1, 1, 0], (partner, head)))
    for copy in last_pair:
        copy.start()
    for copy in last_pair:
        copy.wait_recv()

    for mine in range(2):
        rows = pl.ds(mine * half, half)
        other = pl.ds((1 - mine) * half, half)

        @pl.when(core == mine)
        def _():
            if mine == 0:
                fwd_out[rows, :] = res_f[...]
                fwd_out[other, :] = fin_f[...]
                bwd_out[rows, :] = res_b[...] + peer_b[rows, :]
                bwd_out[other, :] = fin_b[...] + peer_b[other, :]
            else:
                fwd_out[rows, :] = res_f[...] + peer_f[rows, :]
                fwd_out[other, :] = fin_f[...] + peer_f[other, :]
                bwd_out[rows, :] = res_b[...]
                bwd_out[other, :] = fin_b[...]

    for h in range(heads):
        rows = slice(h * dim, (h + 1) * dim)
        running = fwd_out[rows, :]
        for n in range(nblocks):
            block_sum = kv_blk[n, rows, :]
            kv_blk[n, rows, :] = running
            if n + 1 < nblocks:
                running = running + block_sum
        running = bwd_out[rows, :]
        for n in reversed(range(nblocks)):
            block_sum = g_blk[n, rows, :]
            g_blk[n, rows, :] = running
            if n > 0:
                running = running + block_sum

    vm_out = (gq_ref, gk_ref, gv_ref)
    hbm_out = (gq_hbm, gk_hbm, gv_hbm)

    def gather_out(a, j):
        return pltpu.make_async_remote_copy(
            src_ref=vm_out[a].at[pl.ds(j * rows_in, rows_in)],
            dst_ref=hbm_out[a].at[:, pl.ds(head * cols_in, cols_in)],
            send_sem=x_sems.at[0, 4 + a, j], recv_sem=x_sems.at[1, 4 + a, head],
            device_id=(me, j), device_id_type=MESH)

    def gather_out_in(a, j):
        return pltpu.make_async_remote_copy(
            src_ref=vm_out[a].at[pl.ds(j * rows_in, rows_in)],
            dst_ref=hbm_out[a].at[:, pl.ds(j * cols_in, cols_in)],
            send_sem=x_sems.at[0, 4 + a, j], recv_sem=x_sems.at[1, 4 + a, j],
            device_id=(me, j), device_id_type=MESH)

    stores = [pltpu.make_async_copy(vm_out[a].at[pl.ds(head * rows_in, rows_in)],
                                    hbm_out[a].at[:, pl.ds(head * cols_in, cols_in)], io_sems.at[4 + a])
              for a in range(3)]
    per_block = blk // rows_in
    for n in range(nblocks):
        out_rows = slice(n * blk, (n + 1) * blk)
        for h in range(heads):
            rows = slice(h * dim, (h + 1) * dim)
            out_cols = slice(h * dim, (h + 1) * dim)
            kf = cut(k_ref, n, h).astype(jnp.float32)
            vf = cut(v_ref, n, h).astype(jnp.float32)
            df = cut(d_ref, n, h).astype(jnp.float32)
            kv_s = kv_blk[n, rows, :]
            g_s = g_blk[n, rows, :]
            gq_ref[out_rows, out_cols] = (
                scale * (acc_q[out_rows, out_cols] + _split_dot(cut(d_ref, n, h), kv_s))
            ).astype(gq_ref.dtype)
            gk_ref[out_rows, out_cols] = (
                scale * (acc_k[out_rows, out_cols] + _split_dot(cut(v_ref, n, h), g_s))
            ).astype(gk_ref.dtype)
            gv_ref[out_rows, out_cols] = (
                acc_v[out_rows, out_cols] + scale * _split_dot(cut(k_ref, n, h), g_s, tb=True)
            ).astype(gv_ref.dtype)
        for j in range(n * per_block, (n + 1) * per_block):
            for a in range(3):
                @pl.when(head != j)
                def _():
                    gather_out(a, j).start()

                @pl.when(head == j)
                def _():
                    stores[a].start()

    for copy in first + last_pair:
        copy.wait_send()
    for s in range(2):
        for xp in range(plane):
            @pl.when(x != xp)
            def _():
                scatter(s, xp).wait_send()
                gather(s, xp).wait_send()
    for k in range(rounds):
        shift = 1 << k
        up, down = z_copies(k)

        @pl.when(z + shift < planes)
        def _():
            up.wait_send()

        @pl.when(z >= shift)
        def _():
            down.wait_send()
    for copy in stores:
        copy.wait()
    for a in range(4):
        for j in range(ways):
            @pl.when(head != j)
            def _():
                spread_in(a, j).wait_send()
    for a in range(3):
        for j in range(ways):
            @pl.when(head != j)
            def _():
                gather_out_in(a, j).wait_send()
                gather_out_in(a, j).wait_recv()


PLANE = 4
VMEM_ALL = 67043328


def core_math(q_rows, k_rows, v_rows, d_rows):
    count = lax.axis_size("ctx")
    ways = lax.axis_size("head")
    rows_in, full_width = q_rows.shape
    tokens, width = rows_in * ways, full_width // ways
    scale = (HEAD_DIM * tokens * count) ** (-0.5)
    chips = count // 2
    plane = PLANE if chips % PLANE == 0 else 1
    planes = chips // plane
    rounds = max(1, (planes - 1).bit_length())
    heads = width // HEAD_DIM
    nblocks = tokens // GROUP
    rows = heads * HEAD_DIM
    half = rows // 2
    qr = half // plane
    cols = HEAD_DIM
    anywhere = pl.BlockSpec(memory_space=pl.ANY)
    f32 = jnp.float32
    return pl.pallas_call(
        functools.partial(core_kernel, plane, planes, rounds, half, nblocks, heads, scale, ways),
        out_shape=(jax.ShapeDtypeStruct(q_rows.shape, q_rows.dtype),) * 3,
        in_specs=[anywhere] * 4,
        out_specs=(anywhere,) * 3,
        scratch_shapes=[
            *[pltpu.VMEM((tokens, width), q_rows.dtype) for _ in range(7)],
            pltpu.SemaphoreType.DMA((7,)),
            pltpu.VMEM((rows, cols), f32),
            pltpu.VMEM((rows, cols), f32),
            pltpu.VMEM((nblocks, rows, cols), f32),
            pltpu.VMEM((nblocks, rows, cols), f32),
            pltpu.VMEM((tokens, width), f32),
            pltpu.VMEM((tokens, width), f32),
            pltpu.VMEM((tokens, width), f32),
            pltpu.VMEM((rows, cols), f32),
            pltpu.VMEM((rows, cols), f32),
            pltpu.VMEM((half, cols), f32),
            pltpu.VMEM((half, cols), f32),
            pltpu.VMEM((2, plane, qr, cols), f32),
            pltpu.VMEM((2, plane, qr, cols), f32),
            pltpu.VMEM((rounds, qr, cols), f32),
            pltpu.VMEM((rounds, qr, cols), f32),
            pltpu.VMEM((rounds, qr, cols), f32),
            pltpu.VMEM((rounds, qr, cols), f32),
            pltpu.VMEM((qr, cols), f32),
            pltpu.VMEM((qr, cols), f32),
            pltpu.VMEM((2, plane, qr, cols), f32),
            pltpu.VMEM((2, plane, qr, cols), f32),
            pltpu.VMEM((half, cols), f32),
            pltpu.VMEM((half, cols), f32),
            pltpu.VMEM((half, cols), f32),
            pltpu.VMEM((half, cols), f32),
            pltpu.VMEM((rows, cols), f32),
            pltpu.VMEM((rows, cols), f32),
            pltpu.SemaphoreType.DMA((2, 5, 2, max(plane, rounds))),
            pltpu.SemaphoreType.DMA((2, 7, ways)),
        ],
        compiler_params=pltpu.CompilerParams(collective_id=0, has_side_effects=True,
                                             vmem_limit_bytes=VMEM_ALL),
    )(q_rows, k_rows, v_rows, d_rows)


def exchange_kernel(count, n_arrays, src_cut, dst_cut, *refs):
    srcs = refs[:n_arrays]
    dsts = refs[n_arrays:2 * n_arrays]
    send_sems, recv_sems, local_sems = refs[2 * n_arrays:]
    me = lax.axis_index("head")
    place = lax.axis_index("ctx")
    barrier = pltpu.get_barrier_semaphore()
    for j in range(count):
        @pl.when(me != j)
        def _():
            pl.semaphore_signal(barrier, inc=1, device_id=(place, j), device_id_type=MESH)
    pl.semaphore_wait(barrier, count - 1)

    def remote(a, j, dst_index):
        return pltpu.make_async_remote_copy(
            src_ref=src_cut(srcs[a], j), dst_ref=dst_cut(dsts[a], dst_index),
            send_sem=send_sems.at[a, j], recv_sem=recv_sems.at[a, me],
            device_id=(place, j), device_id_type=MESH)

    for a in range(n_arrays):
        local = pltpu.make_async_copy(src_cut(srcs[a], me), dst_cut(dsts[a], me), local_sems.at[a])
        local.start()
    for step in range(1, count):
        for a in range(n_arrays):
            j_dyn = lax.rem(me + step, count)
            for j in range(count):
                @pl.when(j_dyn == j)
                def _():
                    remote(a, j, me).start()
    for a in range(n_arrays):
        pltpu.make_async_copy(src_cut(srcs[a], me), dst_cut(dsts[a], me), local_sems.at[a]).wait()
    for a in range(n_arrays):
        for j in range(count):
            @pl.when(me != j)
            def _():
                copy = pltpu.make_async_remote_copy(
                    src_ref=src_cut(srcs[a], j), dst_ref=dst_cut(dsts[a], j),
                    send_sem=send_sems.at[a, j], recv_sem=recv_sems.at[a, j],
                    device_id=(place, j), device_id_type=MESH)
                copy.wait_send()
                copy.wait_recv()


def exchange(arrays, out_shape, src_cut, dst_cut, collective_id, in_space, out_space):
    count = lax.axis_size("head")
    if count == 1:
        return tuple(arrays)
    n_arrays = len(arrays)
    in_spec = pl.BlockSpec(memory_space=in_space)
    out_spec = pl.BlockSpec(memory_space=out_space)
    return pl.pallas_call(
        functools.partial(exchange_kernel, count, n_arrays, src_cut, dst_cut),
        out_shape=tuple(jax.ShapeDtypeStruct(out_shape, arrays[0].dtype) for _ in arrays),
        in_specs=[in_spec] * n_arrays,
        out_specs=tuple(out_spec for _ in arrays),
        scratch_shapes=[
            pltpu.SemaphoreType.DMA((n_arrays, count)),
            pltpu.SemaphoreType.DMA((n_arrays, count)),
            pltpu.SemaphoreType.DMA((n_arrays,)),
        ],
        compiler_params=pltpu.CompilerParams(collective_id=collective_id, has_side_effects=True,
                                             vmem_limit_bytes=VMEM_ALL),
    )(*arrays)


def per_device(queries, key_rows, value_rows, grad_out):
    return core_math(queries, key_rows, value_rows, grad_out)


def solution(mesh):
    placed = (
        P(("ctx", "head"), None),
        P(("ctx", "head"), None),
        P(("ctx", "head"), None),
        P(("ctx", "head"), None),
    )
    return jax.shard_map(
        per_device,
        mesh=mesh,
        in_specs=placed,
        out_specs=(P(("ctx", "head"), None), P(("ctx", "head"), None), P(("ctx", "head"), None)),
        check_vma=False,
    )
```
